32 devices in a mesh: cfg: 2 (over core), seq: 8 (over z, y), mlp: 2 (over x).
Axes of the slice: x: 2, y: 2, z: 4, core: 2. Of those that a mesh axis runs over, the one named last changes fastest.
Arguments:
- image_hidden: bfloat16 [2, 256, 8, 1536], P('cfg', ('seq', 'mlp')), may hold values from -6 to 6
- text_hidden: bfloat16 [2, 1232, 1536], P('cfg', 'seq'), may hold values from -6 to 6
- modulation: float32 [2, 8, 10, 1536], P('cfg'), may hold values from -3 to 3
- text_lengths: int32 [2, 8], P('cfg'), may hold values from 1 to 154, as said below
- timestep: int32 [1], replicated, may hold values from 0 to 27
- latent: float32 [256, 8, 64], P(('seq', 'mlp'), 'cfg'), may hold values from -6 to 6
- w_qkv: bfloat16 [3, 1536, 1536], P(None, None, 'mlp'), may hold values from -0.15625 to 0.15625
- w_out: bfloat16 [1536, 1536], P('mlp'), may hold values from -0.15625 to 0.15625
- w_text_kv: bfloat16 [2, 1536, 1536], P(None, None, 'mlp'), may hold values from -0.15625 to 0.15625
- norm_gain: float32 [3, 64], replicated, may hold values from 1 to 2
- w_up: bfloat16 [1536, 6144], P(None, 'mlp'), may hold values from -0.15625 to 0.15625
- w_down: bfloat16 [6144, 1536], P('mlp'), may hold values from -0.078125 to 0.078125
- w_head: bfloat16 [1536, 64], replicated, may hold values from -0.078125 to 0.078125
Outputs:
- velocity: float32 [256, 8, 64], P(('seq', 'mlp'), 'cfg')
- next_latent: float32 [256, 8, 64], P(('seq', 'mlp'), 'cfg')
- denoised: float32 [256, 8, 64], P(('seq', 'mlp'), 'cfg')
The draws below stay inside these ranges and needn't reach their ends.
Inputs may be any that keep to these rules, and one draw needn't show every extreme that they name: Text position j of prompt b in half c is a real token only if j < text_lengths[c, b]; in every draw some length equals 154 and some equals 1.
All inputs are finite; a program needn't handle non-finite values.
Results may differ from the reference program's by a relative error of at most 0.0085.
Values may be sent and summed in bfloat16 or wider, within the bound.
A program may use at most 128 MiB of HBM per device.

```python
import math
import jax
import jax.numpy as jnp
from jax import lax

D = 1536
HEADS = 24
HEAD_DIM = 64
MLP_UNITS = 6144
PATCH_CH = 64
PROMPTS = 8
TXT = 154
STEPS = 28
IMG = 256
N_MLP = 2


def draw_text_lengths(key, part):
    first, second, third = jax.random.split(key, 3)
    count = 2 * PROMPTS
    values = jax.random.randint(first, (count,), 1, TXT + 1)
    top_slot = jax.random.randint(second, (), 0, count)
    low_slot = (top_slot + 1 + jax.random.randint(third, (), 0, count - 1)) % count
    values = values.at[top_slot].set(TXT).at[low_slot].set(1)
    return values.reshape(2, PROMPTS).astype(jnp.int32)


def block_levels(rng, shape, pieces, least, high):
    level = 1.0
    for axis_at, parts in pieces:
        draws = jax.random.uniform(jax.random.fold_in(jax.random.fold_in(rng, 6), axis_at), (parts,), jnp.float32, least / len(pieces), high / len(pieces))
        level = level * jnp.repeat(jnp.exp(draws), shape[axis_at] // parts).reshape((-1,) + (1,) * (len(shape) - 1 - axis_at))
    return level


def gaussian(stream_key, shape, scale, most, pieces=(), held_as=jnp.bfloat16):
    result = scale * jax.random.normal(stream_key, shape, jnp.float32)
    if pieces:
        result = result * block_levels(stream_key, shape, pieces, -0.22, 0.18)
    return jnp.clip(result, -most, most).astype(held_as)


def setup_inputs(seed: int = 0) -> dict:
    key_of = jax.random.split(jax.random.key(seed), 14)
    image_hidden = gaussian(key_of[0], (2, IMG, PROMPTS, D), 1.0, 6.0, ((0, 2), (1, 16)))
    text_hidden = gaussian(key_of[1], (2, PROMPTS * TXT, D), 1.0, 6.0, ((0, 2), (1, 8)))
    modulation = gaussian(key_of[2], (2, PROMPTS, 10, D), 0.5, 3.0, ((0, 2),), jnp.float32)
    text_lengths = draw_text_lengths(jax.random.fold_in(key_of[13], 71), 0)
    timestep = jax.random.randint(key_of[4], (1,), 0, STEPS).astype(jnp.int32)
    latent = gaussian(key_of[5], (IMG, PROMPTS, PATCH_CH), 1.0, 6.0, ((0, 16), (1, 2)), jnp.float32)
    w_qkv = gaussian(key_of[6], (3, D, D), D ** -0.5, 0.15625, ((2, 2),))
    w_out = gaussian(key_of[7], (D, D), D ** -0.5, 0.15625, ((0, 2),))
    w_text_kv = gaussian(key_of[8], (2, D, D), D ** -0.5, 0.15625, ((2, 2),))
    norm_gain = jnp.clip(jnp.exp(jax.random.uniform(key_of[9], (3, HEAD_DIM), jnp.float32, math.log(1.0), math.log(2.0))), 1.0, 2.0)
    w_up = gaussian(key_of[10], (D, MLP_UNITS), D ** -0.5, 0.15625, ((1, 2),))
    w_down = gaussian(key_of[11], (MLP_UNITS, D), MLP_UNITS ** -0.5, 0.078125, ((0, 2),))
    w_head = gaussian(key_of[12], (D, PATCH_CH), (4 * D) ** -0.5, 0.078125)
    return {"image_hidden": image_hidden, "text_hidden": text_hidden, "modulation": modulation, "text_lengths": text_lengths, "timestep": timestep, "latent": latent, "w_qkv": w_qkv, "w_out": w_out, "w_text_kv": w_text_kv, "norm_gain": norm_gain, "w_up": w_up, "w_down": w_down, "w_head": w_head}


EPS = 1e-06
GUIDE = 4.5
SHIFT = 3.0

def layer_norm(values):
    mean = lax.optimization_barrier(jnp.mean(values, axis=-1, keepdims=True))
    centred = values - mean
    spread = lax.optimization_barrier(jnp.mean(centred * centred, axis=-1, keepdims=True))
    return centred * lax.rsqrt(spread + EPS)

def modulate(values, shift, scale):
    return layer_norm(values) * (1.0 + scale) + shift

def head_norm(values, gain):
    shaped = values.reshape(values.shape[:-1] + (values.shape[-1] // HEAD_DIM, HEAD_DIM))
    square = lax.optimization_barrier(jnp.mean(shaped * shaped, axis=-1, keepdims=True))
    return (shaped * lax.rsqrt(square + EPS) * gain).astype(jnp.bfloat16)

def grouped_sum(inputs, weight, groups):
    width = inputs.shape[1] // groups

    def add_group(total, group):
        part_in = lax.dynamic_slice_in_dim(inputs, group * width, width, 1)
        part_w = lax.dynamic_slice_in_dim(weight, group * width, width, 0)
        term = jnp.dot(part_in, part_w, preferred_element_type=jnp.float32).astype(jnp.bfloat16)
        term = lax.optimization_barrier(term)
        return (total + term.astype(jnp.float32), None)
    start = jnp.zeros((inputs.shape[0], weight.shape[1]), jnp.float32)
    return lax.scan(add_group, start, jnp.arange(groups, dtype=jnp.int32))[0]

def sigma_of(index):
    level = 1.0 - index.astype(jnp.float32) / STEPS
    return SHIFT * level / (1.0 + (SHIFT - 1.0) * level)

def attend(items):
    query, key_img, value_img, key_txt, value_txt, keep = items
    factor = 1.0 / math.sqrt(HEAD_DIM)
    query_f = query.astype(jnp.float32)
    score_img = jnp.einsum('qhd,khd->hqk', query_f, key_img.astype(jnp.float32)) * factor
    score_txt = jnp.einsum('qhd,khd->hqk', query_f, key_txt.astype(jnp.float32)) * factor
    weight_img = jnp.exp(score_img)
    weight_txt = jnp.exp(score_txt) * keep[None, None, :]
    round_img = lax.optimization_barrier(weight_img.astype(jnp.bfloat16))
    round_txt = lax.optimization_barrier(weight_txt.astype(jnp.bfloat16))
    numer = jnp.einsum('hqk,khd->qhd', round_img.astype(jnp.float32), value_img.astype(jnp.float32))
    numer = numer + jnp.einsum('hqk,khd->qhd', round_txt.astype(jnp.float32), value_txt.astype(jnp.float32))
    denom = lax.optimization_barrier(jnp.sum(weight_img, axis=-1)) + lax.optimization_barrier(jnp.sum(weight_txt, axis=-1))
    return (numer / jnp.transpose(denom)[:, :, None]).astype(jnp.bfloat16)

def half_velocity(hidden, text, mods, lengths, w_qkv, w_out, w_text_kv, norm_gain, w_up, w_down, w_head):
    total_rows = IMG * PROMPTS
    hid = hidden.astype(jnp.float32)
    normed = modulate(hid, mods[:, 0], mods[:, 1]).astype(jnp.bfloat16).reshape(total_rows, D)
    query = head_norm(jnp.dot(normed, w_qkv[0], preferred_element_type=jnp.float32), norm_gain[0])
    query = query.reshape(IMG, PROMPTS, HEADS, HEAD_DIM)
    keys = head_norm(jnp.dot(normed, w_qkv[1], preferred_element_type=jnp.float32), norm_gain[1])
    keys = keys.reshape(IMG, PROMPTS, HEADS, HEAD_DIM)
    values = jnp.dot(normed, w_qkv[2], preferred_element_type=jnp.float32).astype(jnp.bfloat16)
    values = values.reshape(IMG, PROMPTS, HEADS, HEAD_DIM)
    text_f = text.astype(jnp.float32).reshape(PROMPTS, TXT, D)
    text_normed = modulate(text_f, mods[:, 6][:, None], mods[:, 7][:, None]).astype(jnp.bfloat16)
    text_normed = text_normed.reshape(PROMPTS * TXT, D)
    text_keys = head_norm(jnp.dot(text_normed, w_text_kv[0], preferred_element_type=jnp.float32), norm_gain[2])
    text_keys = text_keys.reshape(PROMPTS, TXT, HEADS, HEAD_DIM)
    text_values = jnp.dot(text_normed, w_text_kv[1], preferred_element_type=jnp.float32).astype(jnp.bfloat16)
    text_values = text_values.reshape(PROMPTS, TXT, HEADS, HEAD_DIM)
    keep = (jnp.arange(TXT, dtype=jnp.int32)[None, :] < lengths[:, None]).astype(jnp.float32)
    attended = lax.map(attend, (jnp.transpose(query, (1, 0, 2, 3)), jnp.transpose(keys, (1, 0, 2, 3)), jnp.transpose(values, (1, 0, 2, 3)), text_keys, text_values, keep))
    attended = jnp.transpose(attended, (1, 0, 2, 3)).reshape(total_rows, D)
    attention_out = grouped_sum(attended, w_out, N_MLP).reshape(IMG, PROMPTS, D)
    first = hid + mods[:, 2] * attention_out
    mlp_in = modulate(first, mods[:, 3], mods[:, 4]).astype(jnp.bfloat16).reshape(total_rows, D)
    raised = jnp.dot(mlp_in, w_up, preferred_element_type=jnp.float32)
    activated = jax.nn.gelu(raised, approximate=True).astype(jnp.bfloat16)
    mlp_out = grouped_sum(activated, w_down, N_MLP).reshape(IMG, PROMPTS, D)
    second = first + mods[:, 5] * mlp_out
    final = modulate(second, mods[:, 8], mods[:, 9]).astype(jnp.bfloat16).reshape(total_rows, D)
    return jnp.dot(final, w_head, preferred_element_type=jnp.float32).reshape(IMG, PROMPTS, PATCH_CH)

def reference(image_hidden, text_hidden, modulation, text_lengths, timestep, latent, w_qkv, w_out, w_text_kv, norm_gain, w_up, w_down, w_head):
    halves = []
    for branch in range(2):
        halves.append(half_velocity(image_hidden[branch], text_hidden[branch], modulation[branch], text_lengths[branch], w_qkv, w_out, w_text_kv, norm_gain, w_up, w_down, w_head))
    velocity = halves[1] + GUIDE * (halves[0] - halves[1])
    sigma_now = sigma_of(timestep[0])
    sigma_after = sigma_of(timestep[0] + 1)
    next_latent = latent + (sigma_after - sigma_now) * velocity
    denoised = latent - sigma_now * velocity
    return (velocity, next_latent, denoised)
```

```python
import math

import jax
import jax.numpy as jnp
from jax import lax
from jax.experimental import pallas as pl
from jax.experimental.pallas import tpu as pltpu
from jax.sharding import PartitionSpec as P

HEAD_DIM = 64
TXT = 154
STEPS = 28


EPS = 1e-06
GUIDE = 4.5
SHIFT = 3.0
PROMPTS = 8
PATCH = 64
MESH = pl.DeviceIdType.MESH


def partner_2(block, axis, stride):
    count = lax.axis_size(axis)
    route = []
    for low in range(count):
        high = low | 1 << stride
        if high != low and high < count:
            route += [(low, high), (high, low)]
    return lax.ppermute(block, axis, route)


def layer_norm(values):
    mean = jnp.mean(values, axis=-1, keepdims=True)
    centred = values - mean
    spread = jnp.mean(centred * centred, axis=-1, keepdims=True)
    return centred * lax.rsqrt(spread + EPS)


def modulate(values, shift, scale):
    return layer_norm(values) * (1.0 + scale) + shift


def head_norm(values, gain):
    shaped = values.reshape(values.shape[:-1] + (values.shape[-1] // HEAD_DIM, HEAD_DIM))
    square = jnp.mean(shaped * shaped, axis=-1, keepdims=True)
    return (shaped * lax.rsqrt(square + EPS) * gain).astype(jnp.bfloat16)


def sigma_of(index):
    level = 1.0 - index.astype(jnp.float32) / STEPS
    return SHIFT * level / (1.0 + (SHIFT - 1.0) * level)


def project_image(normed_rows, w_qkv, norm_gain):
    query = head_norm(
        jnp.einsum("tbd,de->tbe", normed_rows, w_qkv[0], preferred_element_type=jnp.float32),
        norm_gain[0],
    )
    keys = head_norm(
        jnp.einsum("tbd,de->tbe", normed_rows, w_qkv[1], preferred_element_type=jnp.float32),
        norm_gain[1],
    )
    values = jnp.einsum(
        "tbd,de->tbe", normed_rows, w_qkv[2], preferred_element_type=jnp.float32
    ).astype(jnp.bfloat16)
    flat_query = query.reshape(query.shape[:-2] + (-1,))
    flat_keys = keys.reshape(keys.shape[:-2] + (-1,))
    return jnp.concatenate([flat_query, flat_keys, values], axis=-1)


def key_terms(query, key_rows, value_rows, keep):
    factor = 1.0 / math.sqrt(HEAD_DIM)
    prompts = query.shape[1]
    if keep is None:
        keep = jnp.ones((prompts, key_rows.shape[0]), jnp.float32)

    def one_prompt(items):
        query_rows, keys_one, values_one, keep_one = items
        scores = (
            jnp.einsum("qhd,khd->hqk", query_rows, keys_one, preferred_element_type=jnp.float32)
            * factor
        )
        weights = jnp.exp(scores) * keep_one[None, None, :]
        numer = jnp.einsum(
            "hqk,khd->hqd",
            weights.astype(jnp.bfloat16),
            values_one,
            preferred_element_type=jnp.float32,
        )
        return (numer, jnp.sum(weights, axis=-1))

    return lax.map(
        one_prompt,
        (
            jnp.moveaxis(query, 1, 0),
            jnp.moveaxis(key_rows, 1, 0),
            jnp.moveaxis(value_rows, 1, 0),
            keep,
        ),
    )


def shards(
    image_hidden,
    text_hidden,
    modulation,
    text_lengths,
    timestep,
    latent,
    w_qkv,
    w_out,
    w_text_kv,
    norm_gain,
    w_up,
    w_down,
    w_head,
):
    mods = modulation[0]
    own_hidden = image_hidden[0]
    rows = own_hidden.shape[0]
    width = w_out.shape[0]
    heads = width // HEAD_DIM
    prompts = mods.shape[0]
    offset = lax.axis_index("mlp") * rows
    block_hidden = lax.all_gather(own_hidden, "mlp", axis=0, tiled=True).astype(jnp.float32)
    normed = modulate(block_hidden, mods[:, 0], mods[:, 1]).astype(jnp.bfloat16)
    projected = project_image(normed, w_qkv, norm_gain)
    block_rows = projected.shape[0]
    query = projected[..., :width].reshape(block_rows, prompts, heads, HEAD_DIM)
    own_pairs = projected[..., width:]
    text_rows = text_hidden.shape[1]
    position = lax.axis_index("seq") * text_rows + lax.iota(jnp.int32, text_rows)
    owner = position // TXT
    pick = (owner[:, None] == lax.iota(jnp.int32, prompts)[None, :]).astype(jnp.float32)
    text_shift = jnp.dot(pick, mods[:, 6], precision=lax.Precision.HIGHEST)
    text_scale = jnp.dot(pick, mods[:, 7], precision=lax.Precision.HIGHEST)
    text_normed = modulate(text_hidden[0].astype(jnp.float32), text_shift, text_scale).astype(
        jnp.bfloat16
    )
    text_keys = head_norm(
        jnp.dot(text_normed, w_text_kv[0], preferred_element_type=jnp.float32), norm_gain[2]
    )
    text_keys = text_keys.reshape(text_rows, width)
    text_values = jnp.dot(text_normed, w_text_kv[1], preferred_element_type=jnp.float32).astype(
        jnp.bfloat16
    )
    text_pairs = jnp.concatenate([text_keys, text_values], axis=-1)
    keep = (lax.iota(jnp.int32, TXT)[None, :] < text_lengths[0][:, None]).astype(jnp.float32)

    def split_pairs(pairs):
        shape = pairs.shape[:2] + (heads, HEAD_DIM)
        return (pairs[..., :width].reshape(shape), pairs[..., width:].reshape(shape))

    all_image, all_text = (
        lax.all_gather(own_pairs, "seq", axis=0, tiled=True),
        lax.all_gather(text_pairs, "seq", axis=0, tiled=True),
    )
    shaped = jnp.transpose(all_text.reshape(prompts, TXT, 2 * width), (1, 0, 2))
    key_rows, value_rows = split_pairs(shaped)
    text_numer, text_denom = key_terms(query, key_rows, value_rows, keep)
    key_rows, value_rows = split_pairs(all_image)
    image_numer, image_denom = key_terms(query, key_rows, value_rows, None)
    numer = text_numer + image_numer
    denom = text_denom + image_denom
    attended = (numer / denom[..., None]).astype(jnp.bfloat16)
    attended = jnp.transpose(attended, (2, 0, 1, 3)).reshape(block_rows, prompts, width)
    part = attended
    attention_out = lax.psum(
        jnp.einsum("tbe,ed->tbd", part, w_out, preferred_element_type=jnp.float32).astype(
            jnp.bfloat16
        ),
        "mlp",
    ).astype(jnp.float32)
    first = block_hidden + mods[:, 2] * attention_out
    mlp_in = modulate(first, mods[:, 3], mods[:, 4]).astype(jnp.bfloat16)
    raised = jnp.einsum("tbd,du->tbu", mlp_in, w_up, preferred_element_type=jnp.float32)
    activated = jax.nn.gelu(raised, approximate=True).astype(jnp.bfloat16)
    own_first = lax.dynamic_slice_in_dim(first, offset, rows, 0)
    part = activated
    mlp_out = lax.psum_scatter(
        jnp.einsum("tbu,ud->tbd", part, w_down, preferred_element_type=jnp.float32).astype(
            jnp.bfloat16
        ),
        "mlp",
        scatter_dimension=0,
        tiled=True,
    ).astype(jnp.float32)
    second = own_first + mods[:, 5] * mlp_out
    final = modulate(second, mods[:, 8], mods[:, 9]).astype(jnp.bfloat16)
    own_velocity = jnp.einsum("tbd,dp->tbp", final, w_head, preferred_element_type=jnp.float32)
    half_count = prompts // 2
    branch = lax.axis_index("cfg")
    outgoing = lax.dynamic_slice_in_dim(own_velocity, (1 - branch) * half_count, half_count, 1)
    kept = lax.dynamic_slice_in_dim(own_velocity, branch * half_count, half_count, 1)
    partner = partner_2(outgoing, "cfg", 0)
    is_conditional = branch == 0
    conditional = jnp.where(is_conditional, kept, partner)
    unconditional = jnp.where(is_conditional, partner, kept)
    velocity = unconditional + GUIDE * (conditional - unconditional)
    sigma_now = sigma_of(timestep[0])
    sigma_after = sigma_of(timestep[0] + 1)
    next_latent = latent + (sigma_after - sigma_now) * velocity
    denoised = latent - sigma_now * velocity
    return (velocity, next_latent, denoised)

def fused_kernel(
    hid_hbm, text_hbm, mod_hbm, len_hbm, step_hbm, latent_hbm, wqkv_hbm, wout_hbm, wtext_hbm,
    gain_hbm, wup_hbm, wdown_hbm, whead_hbm,
    out_ref,
    hid_ref, text_ref, mod_ref, len_ref, step_ref, latent_ref, gain_ref, whead_ref,
    wqkv, wout, wout_far, wtext, wup, wdown,
    wide, ready, gathered, normed, text_norm, q6, k6, v6, kt6, vt6, attended, att_in,
    proj, first_buf, mlp_in, act, down, down_in, final, half_out, half_in,
    isem, wsem, a2a_send, a2a_recv, fwd_send, fwd_recv, far_send, far_recv, at_send, at_recv,
    dn_send, dn_recv, out_send, out_recv,
):
    c = lax.axis_index("cfg")
    s = lax.axis_index("seq")
    m = lax.axis_index("mlp")
    other = 1 - m
    ring = PROMPTS
    rows = hid_ref.shape[0]
    own_rows = rows * ring
    width = wout.shape[0]
    model = wout.shape[1]
    units = wup.shape[1]
    pairs = width // 128
    txt_pad = text_norm.shape[0]
    txt = text_ref.shape[0]
    f32, bf16 = jnp.float32, jnp.bfloat16
    partner = (c, s, other)
    sibling = (1 - c, s, m)

    bits = (lax.rem(s, 2), lax.rem(s // 2, 2), s // 4)

    def peer(k):
        return sum(((1 - bits[i]) if (k >> i) & 1 else bits[i]) * (1 << i) for i in range(3))

    inputs = []
    for i, (src, dst) in enumerate((
        (hid_hbm, hid_ref), (text_hbm, text_ref), (mod_hbm, mod_ref), (gain_hbm, gain_ref),
        (len_hbm, len_ref), (step_hbm, step_ref), (latent_hbm, latent_ref), (whead_hbm, whead_ref),
    )):
        inputs.append(pltpu.make_async_copy(src, dst, isem.at[i]))
    inputs[0].start()

    barrier = pltpu.get_barrier_semaphore()
    for k in range(ring):
        if k:
            pl.semaphore_signal(barrier, inc=1, device_id=(c, peer(k), m), device_id_type=MESH)
        pl.semaphore_signal(barrier, inc=1, device_id=(1 - c, peer(k), m), device_id_type=MESH)
    pl.semaphore_signal(barrier, inc=1, device_id=partner, device_id_type=MESH)

    for cp in inputs[1:]:
        cp.start()
    loads = []
    jobs = [(wtext_hbm.at[i], wtext.at[i]) for i in range(2)]
    jobs += [(wqkv_hbm.at[i], wqkv.at[i]) for i in range(3)]
    jobs += [(wout_hbm, wout)]
    jobs += [(wup_hbm.at[pl.ds(i * model // 2, model // 2)], wup.at[pl.ds(i * model // 2, model // 2)]) for i in range(2)]
    jobs += [(wdown_hbm.at[pl.ds(i * units // 2, units // 2)], wdown.at[pl.ds(i * units // 2, units // 2)]) for i in range(2)]
    for i, (src, dst) in enumerate(jobs):
        loads.append(pltpu.make_async_copy(src, dst, wsem.at[i]))
    for cp in loads[:2]:
        cp.start()

    inputs[0].wait()
    lanes = model // 128
    for j in range(lanes):
        tile = hid_ref[:, :, j * 128 : (j + 1) * 128]
        wide[j] = tile.astype(f32).reshape(own_rows, 128)
    for p in range(ring):
        for j in range(lanes):
            ready[p, :, j * 128 : (j + 1) * 128] = wide[j, pl.ds(p, rows, stride=ring), :].astype(bf16)
    gathered[m, s] = ready[s]
    for cp in inputs[1:]:
        cp.wait()
    for cp in loads[2:5]:
        cp.start()

    def mod_row(k):
        return mod_ref[k, pl.ds(s, 1), :]

    def norm_rows(values, k):
        mean = jnp.mean(values, axis=-1, keepdims=True)
        centred = values - mean
        spread = jnp.mean(centred * centred, axis=-1, keepdims=True)
        return centred * lax.rsqrt(spread + EPS) * (1.0 + mod_row(k + 1)) + mod_row(k)

    whole_blocks = txt // 16

    def text_block(i, carry):
        at = pl.ds(pl.multiple_of(i * 16, 16), 16)
        text_norm[at, :] = norm_rows(text_ref[at, :].astype(f32), 6)
        return carry

    lax.fori_loop(0, whole_blocks, text_block, 0, unroll=3 if whole_blocks % 3 == 0 else 1)
    tail = txt - whole_blocks * 16
    if tail:
        text_norm[whole_blocks * 16 : txt, :] = norm_rows(
            text_ref[whole_blocks * 16 : txt, :].astype(f32), 6)
    if txt_pad > txt:
        text_norm[txt:txt_pad, :] = jnp.zeros((txt_pad - txt, model), f32)

    row_id = lax.broadcasted_iota(jnp.int32, (2 * 128, 128), 0)
    col_id = lax.broadcasted_iota(jnp.int32, (2 * 128, 128), 1)
    same_head = (((row_id // HEAD_DIM) % 2) == (col_id // HEAD_DIM)).astype(f32).astype(bf16)

    def head_norm_tile(u, gain):
        square = u * u
        high = square.astype(bf16)
        low = (square - high.astype(f32)).astype(bf16)
        total = jnp.dot(jnp.concatenate([high, low], axis=1), same_head, preferred_element_type=f32)
        return (u * lax.rsqrt(total * (1.0 / HEAD_DIM) + EPS) * gain).astype(bf16)

    def gain_of(i):
        one = gain_ref[i : i + 1, :]
        return jnp.concatenate([one, one], axis=1)

    keep = (lax.broadcasted_iota(jnp.int32, (txt_pad, 128), 0) < len_ref[0, s]).astype(f32).astype(bf16)
    lane = lax.broadcasted_iota(jnp.int32, (1, 128), 1)
    low_lane = (lane < HEAD_DIM).astype(f32).astype(bf16)
    high_lane = (lane >= HEAD_DIM).astype(f32).astype(bf16)

    def project(lhs, weight, gain, mask, store):
        for j in range(width // 256):
            u = jnp.dot(lhs, weight[:, j * 256 : (j + 1) * 256], preferred_element_type=f32)
            for t in range(2):
                tile = u[:, t * 128 : (t + 1) * 128]
                res = tile.astype(bf16) if gain is None else head_norm_tile(tile, gain)
                store(2 * j + t, res if mask is None else res * mask)

    def to_text(buf):
        def store(i, value):
            buf[i] = value

        return store

    def to_half(buf, half):
        def store(i, value):
            buf[i, half] = value

        return store

    text_lhs = text_norm[...].astype(bf16)
    loads[0].wait()
    project(text_lhs, wtext.at[0], gain_of(2), None, to_text(kt6))
    loads[1].wait()
    project(text_lhs, wtext.at[1], None, keep, to_text(vt6))

    sends = []

    def send(src, dst, ssem, rsem, dev):
        cp = pltpu.make_async_remote_copy(
            src_ref=src, dst_ref=dst, send_sem=ssem, recv_sem=rsem,
            device_id=dev, device_id_type=MESH)
        cp.start()
        sends.append(cp)

    def arrive(dst, ssem, rsem, dev):
        pltpu.make_async_remote_copy(
            src_ref=dst, dst_ref=dst, send_sem=ssem, recv_sem=rsem,
            device_id=dev, device_id_type=MESH).wait_recv()

    pl.semaphore_wait(barrier, 2 * ring)

    for k in (4, 5, 6, 7, 2, 3, 1):
        send(ready.at[peer(k)], gathered.at[m, s], a2a_send.at[k], a2a_recv.at[k], (c, peer(k), m))

    def forward(k):
        src = peer(k)
        if k:
            arrive(gathered.at[m, src], a2a_send.at[k], a2a_recv.at[k], (c, src, m))
        send(gathered.at[m, src], gathered.at[m, src], fwd_send.at[k], fwd_recv.at[k], partner)

    quarter = 4
    piece = width // (4 * quarter)

    def far_rows(core, j, i):
        q0 = (1 - bits[0]) if j & 1 else bits[0]
        q1 = (1 - bits[1]) if j & 2 else bits[1]
        start = (((q0 + 2 * q1) * 2 + core) * 2 + i) * piece
        return pl.ds(pl.multiple_of(start, 16), piece)

    near_y = (c, peer(1), m)
    near_z = (c, peer(2), m)

    def far_send_to(at, i, dev, src=None):
        send((wout_far if src is None else src).at[at], wout_far.at[at], far_send.at[i], far_recv.at[i], dev)

    def far_arrive(at, i, dev):
        arrive(wout_far.at[at], far_send.at[i], far_recv.at[i], dev)

    def far_cross(i):
        far_send_to(far_rows(c, 0, i), i, partner, wout_hbm)

    def far_own(i):
        at = far_rows(c, 0, i)
        far_arrive(at, i, partner)
        far_send_to(at, 4 + i, near_z)
        far_send_to(at, 2 + i, near_y)
        far_send_to(at, 8 + i, sibling)

    def far_from_y(i):
        at = far_rows(c, 1, i)
        far_arrive(at, 2 + i, near_y)
        if i == 0:
            far_send_to(at, 6, near_z)
        far_send_to(at, 10 + i, sibling)

    def far_from_z(i):
        at = far_rows(c, 2, i)
        far_arrive(at, 4 + i, near_z)
        if i == 1:
            far_send_to(at, 7, near_y)
        far_send_to(at, 12 + i, sibling)

    def far_corner(i):
        at = far_rows(c, 3, i)
        far_arrive(at, 6 + i, near_z if i == 0 else near_y)
        far_send_to(at, 14 + i, sibling)

    def far_done():
        for t in range(8):
            far_arrive(far_rows(1 - c, t // 2, t % 2), 8 + t, sibling)

    forward(0)
    far_cross(0)
    far_cross(1)
    for cp in loads[5:]:
        cp.start()

    def norm_blocks(half, first_at, count):
        def block(i, carry):
            normed[half, first_at + i] = norm_rows(gathered[half, first_at + i].astype(f32), 0).astype(bf16)
            return carry

        lax.fori_loop(0, count, block, 0, unroll=2)

    q_gain = gain_of(0) * (1.0 / math.sqrt(HEAD_DIM))
    k_gain = gain_of(1)

    def project_rows(half, which):
        lhs = normed[half].reshape(own_rows, model)
        buf, gain = ((q6, q_gain), (k6, k_gain), (v6, None))[which]
        project(lhs, wqkv.at[which], gain, None, to_half(buf, half))

    forward(1)
    forward(2)
    forward(3)
    forward(4)
    far_own(0)
    forward(5)
    forward(6)
    forward(7)
    norm_blocks(m, 0, ring)
    for i in (2, 3, 4):
        loads[i].wait()
    project_rows(m, 1)
    far_own(1)
    project_rows(m, 2)
    far_from_y(0)
    far_from_z(0)
    project_rows(m, 0)

    for k in range(ring):
        src = peer(k)
        arrive(gathered.at[other, src], fwd_send.at[k], fwd_recv.at[k], partner)
    far_from_y(1)
    far_from_z(1)
    norm_blocks(other, 0, ring)
    project_rows(other, 1)
    project_rows(other, 2)

    def dot_t(a, b):
        return lax.dot_general(a, b, (((1,), (1,)), ((), ())), preferred_element_type=f32)

    def attend_pair(half, p):
        q, kt, vt = q6[p, half], kt6[p], vt6[p]
        k = k6[p].reshape(2 * own_rows, 128)
        v = v6[p].reshape(2 * own_rows, 128)
        outs = []
        for mine, rest in ((low_lane, high_lane), (high_lane, low_lane)):
            qh = q * mine
            w_img = jnp.exp(dot_t(qh, k)).astype(bf16)
            w_txt = jnp.exp(dot_t(qh, kt)).astype(bf16)
            outs.append(
                jnp.dot(w_img, v * mine + rest, preferred_element_type=f32)
                + jnp.dot(w_txt, vt * mine + keep * rest, preferred_element_type=f32))
        numer = jnp.where(lane < HEAD_DIM, outs[0], outs[1])
        denom = pltpu.roll(jnp.where(lane < HEAD_DIM, outs[1], outs[0]), HEAD_DIM, 1)
        attended[half, p // 2, :, (p % 2) * 128 : (p % 2 + 1) * 128] = (numer / denom).astype(bf16)

    def attend(half, base):
        for g in range(pairs // 2):
            for p in (2 * g, 2 * g + 1):
                attend_pair(half, p)
            send(attended.at[half, g], att_in.at[half, g],
                 at_send.at[base + g], at_recv.at[base + g], partner)

    def att_arrive(half, base):
        for g in range(pairs // 2):
            arrive(att_in.at[half, g], at_send.at[base + g], at_recv.at[base + g], partner)

    attend(m, 0)
    project_rows(other, 0)
    far_corner(0)
    far_corner(1)
    attend(other, pairs // 2)
    loads[5].wait()

    def out_rows(half):
        mine = jnp.concatenate([attended[half, g] for g in range(pairs // 2)], axis=1)
        far = jnp.concatenate([att_in[half, g] for g in range(pairs // 2)], axis=1)
        for j in range(model // 512):
            cols = slice(j * 512, (j + 1) * 512)
            res = jnp.dot(mine, wout[:, cols], preferred_element_type=f32)
            res = res + jnp.dot(far, wout_far[:, cols], preferred_element_type=f32)
            proj[:, :, cols] = res.reshape(ring, rows, 512)

    def first_rows(half, hold):
        def block(i, carry):
            first = gathered[half, i].astype(f32) + mod_row(2) * proj[i]
            if hold:
                first_buf[i] = first
            mlp_in[i] = norm_rows(first, 3).astype(bf16)
            return carry

        lax.fori_loop(0, ring, block, 0, unroll=2)

    def up():
        lhs = mlp_in[...].reshape(own_rows, model)
        for j in range(units // 512):
            cols = slice(j * 512, (j + 1) * 512)
            r = jnp.dot(lhs, wup[:, cols], preferred_element_type=f32)
            inner = math.sqrt(2.0 / math.pi) * (r + 0.044715 * (r * r * r))
            act[:, cols] = (0.5 * r * (1.0 + jnp.tanh(inner))).astype(bf16)

    def down_rows(half):
        lhs = act[...]
        for j in range(model // 512):
            cols = slice(j * 512, (j + 1) * 512)
            res = jnp.dot(lhs, wdown[:, cols], preferred_element_type=f32).astype(bf16)
            down[half, :, :, cols] = res.reshape(ring, rows, 512)

    couples = ring // 2

    def couple_at(t):
        b1 = (1 - bits[1]) if t & 1 else bits[1]
        b2 = (1 - bits[2]) if t & 2 else bits[2]
        return 2 * b1 + 4 * b2

    order = tuple(range(couples - 1, -1, -1))

    att_arrive(other, 0)
    far_done()
    out_rows(other)
    first_rows(other, False)
    for i in (6, 7):
        loads[i].wait()
    up()
    for i in (8, 9):
        loads[i].wait()
    down_rows(other)
    for t in order:
        at = pl.ds(couple_at(t), 2)
        send(down.at[other, at], down_in.at[at], dn_send.at[t], dn_recv.at[t], partner)
    att_arrive(m, pairs // 2)
    out_rows(m)
    first_rows(m, True)
    up()
    down_rows(m)

    head = whead_ref[...]
    heads2 = jnp.concatenate([head, head], axis=0)
    home = s // (ring // 2)
    slot = c * (ring // 2) + lax.rem(s, ring // 2)
    at_home = c == home
    outs = []
    for t in order:
        start = couple_at(t)
        at = pl.ds(start, 2)
        arrive(down_in.at[at], dn_send.at[t], dn_recv.at[t], partner)
        for e in range(2):
            i = start + e
            total = down[m, i].astype(f32) + down_in[i].astype(f32)
            second = first_buf[i] + mod_row(5) * total
            final[e] = norm_rows(second, 8).astype(bf16)
        hv = dot_t(final[...].reshape(2 * rows, model), heads2)
        for e in range(2):
            dest = start + e
            half_out[dest] = hv[e * rows : (e + 1) * rows]
            cp = pltpu.make_async_remote_copy(
                src_ref=half_out.at[dest], dst_ref=half_in.at[slot],
                send_sem=out_send.at[2 * t + e], recv_sem=out_recv.at[slot],
                device_id=(home, dest, m), device_id_type=MESH)
            if t:
                cp.start()
                sends.append(cp)
                continue
            stays = jnp.logical_and(at_home, s == dest)
            outs.append((cp, stays))

            @pl.when(jnp.logical_not(stays))
            def _(cp=cp):
                cp.start()

            @pl.when(stays)
            def _(dest=dest):
                half_in[slot] = half_out[dest]

    for q in range(ring):
        branch, local = q // (ring // 2), q % (ring // 2)
        prompt = c * (ring // 2) + local
        is_self = jnp.logical_and(c == branch, s == prompt)

        @pl.when(jnp.logical_not(is_self))
        def _():
            pltpu.make_async_remote_copy(
                src_ref=half_out.at[0], dst_ref=half_in.at[q],
                send_sem=out_send.at[0], recv_sem=out_recv.at[q],
                device_id=(branch, prompt, m), device_id_type=MESH).wait_recv()

    t = jnp.full((1, PATCH), step_ref[0], jnp.int32)

    def sigma(index):
        level = 1.0 - index.astype(f32) / STEPS
        return SHIFT * level / (1.0 + (SHIFT - 1.0) * level)

    now, after = sigma(t), sigma(t + 1)
    for p in range(ring // 2):
        cond = half_in[p][:, :PATCH]
        uncond = half_in[ring // 2 + p][:, :PATCH]
        velocity = uncond + GUIDE * (cond - uncond)
        base = latent_ref[:, p, :]
        out_ref[0, :, p, :] = velocity
        out_ref[1, :, p, :] = base + (after - now) * velocity
        out_ref[2, :, p, :] = base - now * velocity

    for cp in sends:
        cp.wait_send()

    for cp, stays in outs:
        @pl.when(jnp.logical_not(stays))
        def _(cp=cp):
            cp.wait_send()


def fused_shards(
    image_hidden, text_hidden, modulation, text_lengths, timestep, latent,
    w_qkv, w_out, w_text_kv, norm_gain, w_up, w_down, w_head,
):
    f32, bf16 = jnp.float32, jnp.bfloat16
    rows, prompts, model = image_hidden.shape[1:]
    txt = text_hidden.shape[1]
    txt_pad = -(-txt // 16) * 16
    width = w_out.shape[0]
    units = w_up.shape[1]
    own_rows = rows * prompts
    pairs = width // 128
    vmem = pl.BlockSpec(memory_space=pltpu.VMEM)
    anym = pl.BlockSpec(memory_space=pl.ANY)
    dma = pltpu.SemaphoreType.DMA
    out = jax.ShapeDtypeStruct((3,) + latent.shape, f32)
    mods = jnp.transpose(modulation[0], (1, 0, 2))
    head = jnp.transpose(w_head)
    scratch = [
        pltpu.VMEM((rows, prompts, model), bf16),
        pltpu.VMEM((txt, model), bf16),
        pltpu.VMEM(mods.shape, f32),
        pltpu.SMEM(text_lengths.shape, jnp.int32),
        pltpu.SMEM(timestep.shape, jnp.int32),
        pltpu.VMEM(latent.shape, f32),
        pltpu.VMEM(norm_gain.shape, f32),
        pltpu.VMEM(head.shape, bf16),
        pltpu.VMEM(w_qkv.shape, bf16), pltpu.VMEM(w_out.shape, bf16), pltpu.VMEM(w_out.shape, bf16),
        pltpu.VMEM(w_text_kv.shape, bf16),
        pltpu.VMEM(w_up.shape, bf16), pltpu.VMEM(w_down.shape, bf16),
        pltpu.VMEM((model // 128, own_rows, 128), f32),
        pltpu.VMEM((prompts, rows, model), bf16),
        pltpu.VMEM((2, prompts, rows, model), bf16),
        pltpu.VMEM((2, prompts, rows, model), bf16),
        pltpu.VMEM((txt_pad, model), f32),
        pltpu.VMEM((pairs, 2, own_rows, 128), bf16),
        pltpu.VMEM((pairs, 2, own_rows, 128), bf16),
        pltpu.VMEM((pairs, 2, own_rows, 128), bf16),
        pltpu.VMEM((pairs, txt_pad, 128), bf16),
        pltpu.VMEM((pairs, txt_pad, 128), bf16),
        pltpu.VMEM((2, pairs // 2, own_rows, 256), bf16),
        pltpu.VMEM((2, pairs // 2, own_rows, 256), bf16),
        pltpu.VMEM((prompts, rows, model), f32),
        pltpu.VMEM((prompts, rows, model), f32),
        pltpu.VMEM((prompts, rows, model), bf16),
        pltpu.VMEM((own_rows, units), bf16),
        pltpu.VMEM((2, prompts, rows, model), bf16),
        pltpu.VMEM((prompts, rows, model), bf16),
        pltpu.VMEM((2, rows, model), bf16),
        pltpu.VMEM((prompts, rows, 128), f32),
        pltpu.VMEM((prompts, rows, 128), f32),
        dma((8,)), dma((10,)), dma((prompts,)), dma((prompts,)), dma((prompts,)), dma((prompts,)),
        dma((16,)), dma((16,)), dma((pairs,)), dma((pairs,)), dma((prompts // 2,)), dma((prompts // 2,)),
        dma((prompts,)), dma((prompts,)),
    ]
    stacked = pl.pallas_call(
        fused_kernel,
        out_shape=out,
        in_specs=[anym] * 13,
        out_specs=vmem,
        scratch_shapes=scratch,
        compiler_params=pltpu.CompilerParams(
            collective_id=0, has_side_effects=True, vmem_limit_bytes=60 << 20),
        name="fused_block",
    )(
        image_hidden[0], text_hidden[0], mods, text_lengths,
        timestep, latent, w_qkv, w_out, w_text_kv, norm_gain, w_up, w_down, head,
    )
    return stacked[0], stacked[1], stacked[2]


def solution(mesh):
    placed = (
        P("cfg", ("seq", "mlp"), None, None),
        P("cfg", "seq", None),
        P("cfg", None, None, None),
        P("cfg", None),
        P(),
        P(("seq", "mlp"), "cfg", None),
        P(None, None, "mlp"),
        P("mlp", None),
        P(None, None, "mlp"),
        P(),
        P(None, "mlp"),
        P("mlp", None),
        P(),
    )
    fits = mesh.shape["cfg"] == 2 and mesh.shape["seq"] == PROMPTS and mesh.shape["mlp"] == 2
    return jax.shard_map(
        fused_shards if fits else shards,
        mesh=mesh,
        in_specs=placed,
        out_specs=(
            P(("seq", "mlp"), "cfg", None),
            P(("seq", "mlp"), "cfg", None),
            P(("seq", "mlp"), "cfg", None),
        ),
        check_vma=False,
    )
```

```python
import math

import jax
import jax.numpy as jnp
from jax import lax
from jax.experimental import pallas as pl
from jax.experimental.pallas import tpu as pltpu
from jax.sharding import PartitionSpec as P

HEAD_DIM = 64
TXT = 154
STEPS = 28


EPS = 1e-06
GUIDE = 4.5
SHIFT = 3.0
PROMPTS = 8
PATCH = 64
MESH = pl.DeviceIdType.MESH


def partner_2(block, axis, stride):
    count = lax.axis_size(axis)
    route = []
    for low in range(count):
        high = low | 1 << stride
        if high != low and high < count:
            route += [(low, high), (high, low)]
    return lax.ppermute(block, axis, route)


def layer_norm(values):
    mean = jnp.mean(values, axis=-1, keepdims=True)
    centred = values - mean
    spread = jnp.mean(centred * centred, axis=-1, keepdims=True)
    return centred * lax.rsqrt(spread + EPS)


def modulate(values, shift, scale):
    return layer_norm(values) * (1.0 + scale) + shift


def head_norm(values, gain):
    shaped = values.reshape(values.shape[:-1] + (values.shape[-1] // HEAD_DIM, HEAD_DIM))
    square = jnp.mean(shaped * shaped, axis=-1, keepdims=True)
    return (shaped * lax.rsqrt(square + EPS) * gain).astype(jnp.bfloat16)


def sigma_of(index):
    level = 1.0 - index.astype(jnp.float32) / STEPS
    return SHIFT * level / (1.0 + (SHIFT - 1.0) * level)


def project_image(normed_rows, w_qkv, norm_gain):
    query = head_norm(
        jnp.einsum("tbd,de->tbe", normed_rows, w_qkv[0], preferred_element_type=jnp.float32),
        norm_gain[0],
    )
    keys = head_norm(
        jnp.einsum("tbd,de->tbe", normed_rows, w_qkv[1], preferred_element_type=jnp.float32),
        norm_gain[1],
    )
    values = jnp.einsum(
        "tbd,de->tbe", normed_rows, w_qkv[2], preferred_element_type=jnp.float32
    ).astype(jnp.bfloat16)
    flat_query = query.reshape(query.shape[:-2] + (-1,))
    flat_keys = keys.reshape(keys.shape[:-2] + (-1,))
    return jnp.concatenate([flat_query, flat_keys, values], axis=-1)


def key_terms(query, key_rows, value_rows, keep):
    factor = 1.0 / math.sqrt(HEAD_DIM)
    prompts = query.shape[1]
    if keep is None:
        keep = jnp.ones((prompts, key_rows.shape[0]), jnp.float32)

    def one_prompt(items):
        query_rows, keys_one, values_one, keep_one = items
        scores = (
            jnp.einsum("qhd,khd->hqk", query_rows, keys_one, preferred_element_type=jnp.float32)
            * factor
        )
        weights = jnp.exp(scores) * keep_one[None, None, :]
        numer = jnp.einsum(
            "hqk,khd->hqd",
            weights.astype(jnp.bfloat16),
            values_one,
            preferred_element_type=jnp.float32,
        )
        return (numer, jnp.sum(weights, axis=-1))

    return lax.map(
        one_prompt,
        (
            jnp.moveaxis(query, 1, 0),
            jnp.moveaxis(key_rows, 1, 0),
            jnp.moveaxis(value_rows, 1, 0),
            keep,
        ),
    )


def shards(
    image_hidden,
    text_hidden,
    modulation,
    text_lengths,
    timestep,
    latent,
    w_qkv,
    w_out,
    w_text_kv,
    norm_gain,
    w_up,
    w_down,
    w_head,
):
    mods = modulation[0]
    own_hidden = image_hidden[0]
    rows = own_hidden.shape[0]
    width = w_out.shape[0]
    heads = width // HEAD_DIM
    prompts = mods.shape[0]
    offset = lax.axis_index("mlp") * rows
    block_hidden = lax.all_gather(own_hidden, "mlp", axis=0, tiled=True).astype(jnp.float32)
    normed = modulate(block_hidden, mods[:, 0], mods[:, 1]).astype(jnp.bfloat16)
    projected = project_image(normed, w_qkv, norm_gain)
    block_rows = projected.shape[0]
    query = projected[..., :width].reshape(block_rows, prompts, heads, HEAD_DIM)
    own_pairs = projected[..., width:]
    text_rows = text_hidden.shape[1]
    position = lax.axis_index("seq") * text_rows + lax.iota(jnp.int32, text_rows)
    owner = position // TXT
    pick = (owner[:, None] == lax.iota(jnp.int32, prompts)[None, :]).astype(jnp.float32)
    text_shift = jnp.dot(pick, mods[:, 6], precision=lax.Precision.HIGHEST)
    text_scale = jnp.dot(pick, mods[:, 7], precision=lax.Precision.HIGHEST)
    text_normed = modulate(text_hidden[0].astype(jnp.float32), text_shift, text_scale).astype(
        jnp.bfloat16
    )
    text_keys = head_norm(
        jnp.dot(text_normed, w_text_kv[0], preferred_element_type=jnp.float32), norm_gain[2]
    )
    text_keys = text_keys.reshape(text_rows, width)
    text_values = jnp.dot(text_normed, w_text_kv[1], preferred_element_type=jnp.float32).astype(
        jnp.bfloat16
    )
    text_pairs = jnp.concatenate([text_keys, text_values], axis=-1)
    keep = (lax.iota(jnp.int32, TXT)[None, :] < text_lengths[0][:, None]).astype(jnp.float32)

    def split_pairs(pairs):
        shape = pairs.shape[:2] + (heads, HEAD_DIM)
        return (pairs[..., :width].reshape(shape), pairs[..., width:].reshape(shape))

    all_image, all_text = (
        lax.all_gather(own_pairs, "seq", axis=0, tiled=True),
        lax.all_gather(text_pairs, "seq", axis=0, tiled=True),
    )
    shaped = jnp.transpose(all_text.reshape(prompts, TXT, 2 * width), (1, 0, 2))
    key_rows, value_rows = split_pairs(shaped)
    text_numer, text_denom = key_terms(query, key_rows, value_rows, keep)
    key_rows, value_rows = split_pairs(all_image)
    image_numer, image_denom = key_terms(query, key_rows, value_rows, None)
    numer = text_numer + image_numer
    denom = text_denom + image_denom
    attended = (numer / denom[..., None]).astype(jnp.bfloat16)
    attended = jnp.transpose(attended, (2, 0, 1, 3)).reshape(block_rows, prompts, width)
    part = attended
    attention_out = lax.psum(
        jnp.einsum("tbe,ed->tbd", part, w_out, preferred_element_type=jnp.float32).astype(
            jnp.bfloat16
        ),
        "mlp",
    ).astype(jnp.float32)
    first = block_hidden + mods[:, 2] * attention_out
    mlp_in = modulate(first, mods[:, 3], mods[:, 4]).astype(jnp.bfloat16)
    raised = jnp.einsum("tbd,du->tbu", mlp_in, w_up, preferred_element_type=jnp.float32)
    activated = jax.nn.gelu(raised, approximate=True).astype(jnp.bfloat16)
    own_first = lax.dynamic_slice_in_dim(first, offset, rows, 0)
    part = activated
    mlp_out = lax.psum_scatter(
        jnp.einsum("tbu,ud->tbd", part, w_down, preferred_element_type=jnp.float32).astype(
            jnp.bfloat16
        ),
        "mlp",
        scatter_dimension=0,
        tiled=True,
    ).astype(jnp.float32)
    second = own_first + mods[:, 5] * mlp_out
    final = modulate(second, mods[:, 8], mods[:, 9]).astype(jnp.bfloat16)
    own_velocity = jnp.einsum("tbd,dp->tbp", final, w_head, preferred_element_type=jnp.float32)
    half_count = prompts // 2
    branch = lax.axis_index("cfg")
    outgoing = lax.dynamic_slice_in_dim(own_velocity, (1 - branch) * half_count, half_count, 1)
    kept = lax.dynamic_slice_in_dim(own_velocity, branch * half_count, half_count, 1)
    partner = partner_2(outgoing, "cfg", 0)
    is_conditional = branch == 0
    conditional = jnp.where(is_conditional, kept, partner)
    unconditional = jnp.where(is_conditional, partner, kept)
    velocity = unconditional + GUIDE * (conditional - unconditional)
    sigma_now = sigma_of(timestep[0])
    sigma_after = sigma_of(timestep[0] + 1)
    next_latent = latent + (sigma_after - sigma_now) * velocity
    denoised = latent - sigma_now * velocity
    return (velocity, next_latent, denoised)

def fused_kernel(
    hid_hbm, text_hbm, mod_hbm, len_hbm, step_hbm, latent_hbm, wqkv_hbm, wout_hbm, wtext_hbm,
    gain_hbm, wup_hbm, wdown_hbm, whead_hbm,
    out_ref,
    hid_ref, text_ref, mod_ref, len_ref, step_ref, latent_ref, gain_ref, whead_ref,
    wqkv, wout, wout_far, wtext, wup, wdown,
    wide, ready, gathered, normed, text_norm, q6, k6, v6, kt6, vt6, attended, att_in,
    proj, first_buf, mlp_in, act, down, down_in, final, half_out, half_in,
    isem, wsem, a2a_send, a2a_recv, fwd_send, fwd_recv, far_send, far_recv, at_send, at_recv,
    dn_send, dn_recv, out_send, out_recv,
):
    c = lax.axis_index("cfg")
    s = lax.axis_index("seq")
    m = lax.axis_index("mlp")
    other = 1 - m
    ring = PROMPTS
    rows = hid_ref.shape[0]
    own_rows = rows * ring
    width = wout.shape[0]
    model = wout.shape[1]
    units = wup.shape[1]
    pairs = width // 128
    txt_pad = text_norm.shape[0]
    txt = text_ref.shape[0]
    f32, bf16 = jnp.float32, jnp.bfloat16
    partner = (c, s, other)
    sibling = (1 - c, s, m)

    bits = (lax.rem(s, 2), lax.rem(s // 2, 2), s // 4)

    def peer(k):
        return sum(((1 - bits[i]) if (k >> i) & 1 else bits[i]) * (1 << i) for i in range(3))

    inputs = []
    for i, (src, dst) in enumerate((
        (hid_hbm, hid_ref), (text_hbm, text_ref), (mod_hbm, mod_ref), (gain_hbm, gain_ref),
        (len_hbm, len_ref), (step_hbm, step_ref), (latent_hbm, latent_ref), (whead_hbm, whead_ref),
    )):
        inputs.append(pltpu.make_async_copy(src, dst, isem.at[i]))
    inputs[0].start()

    barrier = pltpu.get_barrier_semaphore()
    for k in range(ring):
        if k:
            pl.semaphore_signal(barrier, inc=1, device_id=(c, peer(k), m), device_id_type=MESH)
        pl.semaphore_signal(barrier, inc=1, device_id=(1 - c, peer(k), m), device_id_type=MESH)
    pl.semaphore_signal(barrier, inc=1, device_id=partner, device_id_type=MESH)

    for cp in inputs[1:]:
        cp.start()
    loads = []
    jobs = [(wtext_hbm.at[i], wtext.at[i]) for i in range(2)]
    jobs += [(wqkv_hbm.at[i], wqkv.at[i]) for i in range(3)]
    jobs += [(wout_hbm, wout)]
    jobs += [(wup_hbm.at[pl.ds(i * model // 2, model // 2)], wup.at[pl.ds(i * model // 2, model // 2)]) for i in range(2)]
    jobs += [(wdown_hbm.at[pl.ds(i * units // 2, units // 2)], wdown.at[pl.ds(i * units // 2, units // 2)]) for i in range(2)]
    for i, (src, dst) in enumerate(jobs):
        loads.append(pltpu.make_async_copy(src, dst, wsem.at[i]))
    for cp in loads[:2]:
        cp.start()

    inputs[0].wait()
    lanes = model // 128
    for j in range(lanes):
        tile = hid_ref[:, :, j * 128 : (j + 1) * 128]
        wide[j] = tile.astype(f32).reshape(own_rows, 128)
    for p in range(ring):
        for j in range(lanes):
            ready[p, :, j * 128 : (j + 1) * 128] = wide[j, pl.ds(p, rows, stride=ring), :].astype(bf16)
    gathered[m, s] = ready[s]
    for cp in inputs[1:]:
        cp.wait()
    for cp in loads[2:5]:
        cp.start()

    def mod_row(k):
        return mod_ref[k, pl.ds(s, 1), :]

    def norm_rows(values, k):
        mean = jnp.mean(values, axis=-1, keepdims=True)
        centred = values - mean
        spread = jnp.mean(centred * centred, axis=-1, keepdims=True)
        return centred * lax.rsqrt(spread + EPS) * (1.0 + mod_row(k + 1)) + mod_row(k)

    whole_blocks = txt // 16

    def text_block(i, carry):
        at = pl.ds(pl.multiple_of(i * 16, 16), 16)
        text_norm[at, :] = norm_rows(text_ref[at, :].astype(f32), 6)
        return carry

    lax.fori_loop(0, whole_blocks, text_block, 0, unroll=3 if whole_blocks % 3 == 0 else 1)
    tail = txt - whole_blocks * 16
    if tail:
        text_norm[whole_blocks * 16 : txt, :] = norm_rows(
            text_ref[whole_blocks * 16 : txt, :].astype(f32), 6)
    if txt_pad > txt:
        text_norm[txt:txt_pad, :] = jnp.zeros((txt_pad - txt, model), f32)

    row_id = lax.broadcasted_iota(jnp.int32, (256, 256), 0)
    col_id = lax.broadcasted_iota(jnp.int32, (256, 256), 1)
    same_head = ((row_id // HEAD_DIM) == (col_id // HEAD_DIM)).astype(f32).astype(bf16)

    def square_sums(u):
        return jnp.dot((u * u).astype(bf16), same_head, preferred_element_type=f32)

    def gain_of(i):
        one = gain_ref[i : i + 1, :]
        return jnp.concatenate([one] * 4, axis=1)

    keep = (lax.broadcasted_iota(jnp.int32, (txt_pad, 128), 0) < len_ref[0, s]).astype(f32).astype(bf16)
    lane = lax.broadcasted_iota(jnp.int32, (1, 128), 1)
    low_lane = (lane < HEAD_DIM).astype(f32).astype(bf16)
    high_lane = (lane >= HEAD_DIM).astype(f32).astype(bf16)

    def project(lhs, weight, gain, mask, store):
        blocks = [
            jnp.dot(lhs, weight[:, j * 256 : (j + 1) * 256], preferred_element_type=f32)
            for j in range(width // 256)]
        if gain is not None:
            totals = [square_sums(u) for u in blocks]
            blocks = [
                u * lax.rsqrt(total * (1.0 / HEAD_DIM) + EPS) * gain
                for u, total in zip(blocks, totals)]
        for j, u in enumerate(blocks):
            for t in range(2):
                res = u[:, t * 128 : (t + 1) * 128].astype(bf16)
                store(2 * j + t, res if mask is None else res * mask)

    def to_text(buf):
        def store(i, value):
            buf[i] = value

        return store

    def to_half(buf, half):
        def store(i, value):
            buf[i, half] = value

        return store

    text_lhs = text_norm[...].astype(bf16)
    loads[0].wait()
    project(text_lhs, wtext.at[0], gain_of(2), None, to_text(kt6))
    loads[1].wait()
    project(text_lhs, wtext.at[1], None, keep, to_text(vt6))

    sends = []

    def send(src, dst, ssem, rsem, dev):
        cp = pltpu.make_async_remote_copy(
            src_ref=src, dst_ref=dst, send_sem=ssem, recv_sem=rsem,
            device_id=dev, device_id_type=MESH)
        cp.start()
        sends.append(cp)

    def arrive(dst, ssem, rsem, dev):
        pltpu.make_async_remote_copy(
            src_ref=dst, dst_ref=dst, send_sem=ssem, recv_sem=rsem,
            device_id=dev, device_id_type=MESH).wait_recv()

    pl.semaphore_wait(barrier, 2 * ring)

    for k in (4, 5, 6, 7, 2, 3, 1):
        send(ready.at[peer(k)], gathered.at[m, s], a2a_send.at[k], a2a_recv.at[k], (c, peer(k), m))

    def forward(k):
        src = peer(k)
        if k:
            arrive(gathered.at[m, src], a2a_send.at[k], a2a_recv.at[k], (c, src, m))
        send(gathered.at[m, src], gathered.at[m, src], fwd_send.at[k], fwd_recv.at[k], partner)

    quarter = 4
    piece = width // (4 * quarter)

    def far_rows(core, j, i):
        q0 = (1 - bits[0]) if j & 1 else bits[0]
        q1 = (1 - bits[1]) if j & 2 else bits[1]
        start = (((q0 + 2 * q1) * 2 + core) * 2 + i) * piece
        return pl.ds(pl.multiple_of(start, 16), piece)

    near_y = (c, peer(1), m)
    near_z = (c, peer(2), m)

    def far_send_to(at, i, dev, src=None):
        send((wout_far if src is None else src).at[at], wout_far.at[at], far_send.at[i], far_recv.at[i], dev)

    def far_arrive(at, i, dev):
        arrive(wout_far.at[at], far_send.at[i], far_recv.at[i], dev)

    def far_cross(i):
        far_send_to(far_rows(c, 0, i), i, partner, wout_hbm)

    def far_own(i):
        at = far_rows(c, 0, i)
        far_arrive(at, i, partner)
        far_send_to(at, 4 + i, near_z)
        far_send_to(at, 2 + i, near_y)
        far_send_to(at, 8 + i, sibling)

    def far_from_y(i):
        at = far_rows(c, 1, i)
        far_arrive(at, 2 + i, near_y)
        if i == 0:
            far_send_to(at, 6, near_z)
        far_send_to(at, 10 + i, sibling)

    def far_from_z(i):
        at = far_rows(c, 2, i)
        far_arrive(at, 4 + i, near_z)
        if i == 1:
            far_send_to(at, 7, near_y)
        far_send_to(at, 12 + i, sibling)

    def far_corner(i):
        at = far_rows(c, 3, i)
        far_arrive(at, 6 + i, near_z if i == 0 else near_y)
        far_send_to(at, 14 + i, sibling)

    def far_done():
        for t in range(8):
            far_arrive(far_rows(1 - c, t // 2, t % 2), 8 + t, sibling)

    forward(0)
    far_cross(0)
    far_cross(1)
    for cp in loads[5:]:
        cp.start()

    def norm_blocks(half, first_at, count):
        def block(i, carry):
            normed[half, first_at + i] = norm_rows(gathered[half, first_at + i].astype(f32), 0).astype(bf16)
            return carry

        lax.fori_loop(0, count, block, 0, unroll=count)

    q_gain = gain_of(0) * (1.0 / math.sqrt(HEAD_DIM))
    k_gain = gain_of(1)

    def project_rows(half, which):
        lhs = normed[half].reshape(own_rows, model)
        buf, gain = ((q6, q_gain), (k6, k_gain), (v6, None))[which]
        project(lhs, wqkv.at[which], gain, None, to_half(buf, half))

    forward(1)
    forward(2)
    forward(3)
    forward(4)
    far_own(0)
    forward(5)
    forward(6)
    forward(7)
    norm_blocks(m, 0, ring)
    for i in (2, 3, 4):
        loads[i].wait()
    project_rows(m, 1)
    far_own(1)
    project_rows(m, 2)
    far_from_y(0)
    far_from_z(0)
    project_rows(m, 0)

    for k in range(ring):
        src = peer(k)
        arrive(gathered.at[other, src], fwd_send.at[k], fwd_recv.at[k], partner)
    far_from_y(1)
    far_from_z(1)
    norm_blocks(other, 0, ring)
    project_rows(other, 1)
    project_rows(other, 2)

    def dot_t(a, b):
        return lax.dot_general(a, b, (((1,), (1,)), ((), ())), preferred_element_type=f32)

    def attend_pair(half, p):
        q, kt, vt = q6[p, half], kt6[p], vt6[p]
        k = k6[p].reshape(2 * own_rows, 128)
        v = v6[p].reshape(2 * own_rows, 128)
        outs = []
        for mine, rest in ((low_lane, high_lane), (high_lane, low_lane)):
            qh = q * mine
            w_img = jnp.exp(dot_t(qh, k)).astype(bf16)
            w_txt = jnp.exp(dot_t(qh, kt)).astype(bf16)
            outs.append(
                jnp.dot(w_img, v * mine + rest, preferred_element_type=f32)
                + jnp.dot(w_txt, vt * mine + keep * rest, preferred_element_type=f32))
        numer = jnp.where(lane < HEAD_DIM, outs[0], outs[1])
        denom = pltpu.roll(jnp.where(lane < HEAD_DIM, outs[1], outs[0]), HEAD_DIM, 1)
        attended[half, p // 2, :, (p % 2) * 128 : (p % 2 + 1) * 128] = (numer / denom).astype(bf16)

    def attend(half, base):
        for g in range(pairs // 2):
            for p in (2 * g, 2 * g + 1):
                attend_pair(half, p)
            send(attended.at[half, g], att_in.at[half, g],
                 at_send.at[base + g], at_recv.at[base + g], partner)

    def att_arrive(half, base):
        for g in range(pairs // 2):
            arrive(att_in.at[half, g], at_send.at[base + g], at_recv.at[base + g], partner)

    attend(m, 0)
    project_rows(other, 0)
    far_corner(0)
    far_corner(1)
    attend(other, pairs // 2)
    loads[5].wait()

    def out_rows(half):
        mine = jnp.concatenate([attended[half, g] for g in range(pairs // 2)], axis=1)
        far = jnp.concatenate([att_in[half, g] for g in range(pairs // 2)], axis=1)
        for j in range(model // 512):
            cols = slice(j * 512, (j + 1) * 512)
            res = jnp.dot(mine, wout[:, cols], preferred_element_type=f32)
            res = res + jnp.dot(far, wout_far[:, cols], preferred_element_type=f32)
            proj[:, :, cols] = res.reshape(ring, rows, 512)

    def first_rows(half, hold):
        def block(i, carry):
            first = gathered[half, i].astype(f32) + mod_row(2) * proj[i]
            if hold:
                first_buf[i] = first
            mlp_in[i] = norm_rows(first, 3).astype(bf16)
            return carry

        lax.fori_loop(0, ring, block, 0, unroll=ring)

    def up():
        lhs = mlp_in[...].reshape(own_rows, model)
        for j in range(units // 512):
            cols = slice(j * 512, (j + 1) * 512)
            r = jnp.dot(lhs, wup[:, cols], preferred_element_type=f32)
            inner = math.sqrt(2.0 / math.pi) * (r + 0.044715 * (r * r * r))
            act[:, cols] = (0.5 * r * (1.0 + jnp.tanh(inner))).astype(bf16)

    def down_rows(half):
        lhs = act[...]
        for j in range(model // 512):
            cols = slice(j * 512, (j + 1) * 512)
            res = jnp.dot(lhs, wdown[:, cols], preferred_element_type=f32).astype(bf16)
            down[half, :, :, cols] = res.reshape(ring, rows, 512)

    couples = ring // 2

    def couple_at(t):
        b1 = (1 - bits[1]) if t & 1 else bits[1]
        b2 = (1 - bits[2]) if t & 2 else bits[2]
        return 2 * b1 + 4 * b2

    order = tuple(range(couples - 1, -1, -1))

    att_arrive(other, 0)
    far_done()
    out_rows(other)
    first_rows(other, False)
    for i in (6, 7):
        loads[i].wait()
    up()
    for i in (8, 9):
        loads[i].wait()
    down_rows(other)
    for t in order:
        at = pl.ds(couple_at(t), 2)
        send(down.at[other, at], down_in.at[at], dn_send.at[t], dn_recv.at[t], partner)
    att_arrive(m, pairs // 2)
    out_rows(m)
    first_rows(m, True)
    up()
    down_rows(m)

    head = whead_ref[...]
    heads2 = jnp.concatenate([head, head], axis=0)
    home = s // (ring // 2)
    slot = c * (ring // 2) + lax.rem(s, ring // 2)
    at_home = c == home
    outs = []
    for t in order:
        start = couple_at(t)
        at = pl.ds(start, 2)
        arrive(down_in.at[at], dn_send.at[t], dn_recv.at[t], partner)
        for e in range(2):
            i = start + e
            total = down[m, i].astype(f32) + down_in[i].astype(f32)
            second = first_buf[i] + mod_row(5) * total
            final[e] = norm_rows(second, 8).astype(bf16)
        hv = dot_t(final[...].reshape(2 * rows, model), heads2)
        for e in range(2):
            dest = start + e
            half_out[dest] = hv[e * rows : (e + 1) * rows]
            cp = pltpu.make_async_remote_copy(
                src_ref=half_out.at[dest], dst_ref=half_in.at[slot],
                send_sem=out_send.at[2 * t + e], recv_sem=out_recv.at[slot],
                device_id=(home, dest, m), device_id_type=MESH)
            if t:
                cp.start()
                sends.append(cp)
                continue
            stays = jnp.logical_and(at_home, s == dest)
            outs.append((cp, stays))

            @pl.when(jnp.logical_not(stays))
            def _(cp=cp):
                cp.start()

            @pl.when(stays)
            def _(dest=dest):
                half_in[slot] = half_out[dest]

    for q in range(ring):
        branch, local = q // (ring // 2), q % (ring // 2)
        prompt = c * (ring // 2) + local
        is_self = jnp.logical_and(c == branch, s == prompt)

        @pl.when(jnp.logical_not(is_self))
        def _():
            pltpu.make_async_remote_copy(
                src_ref=half_out.at[0], dst_ref=half_in.at[q],
                send_sem=out_send.at[0], recv_sem=out_recv.at[q],
                device_id=(branch, prompt, m), device_id_type=MESH).wait_recv()

    t = jnp.full((1, PATCH), step_ref[0], jnp.int32)

    def sigma(index):
        level = 1.0 - index.astype(f32) / STEPS
        return SHIFT * level / (1.0 + (SHIFT - 1.0) * level)

    now, after = sigma(t), sigma(t + 1)
    for p in range(ring // 2):
        cond = half_in[p][:, :PATCH]
        uncond = half_in[ring // 2 + p][:, :PATCH]
        velocity = uncond + GUIDE * (cond - uncond)
        base = latent_ref[:, p, :]
        out_ref[0, :, p, :] = velocity
        out_ref[1, :, p, :] = base + (after - now) * velocity
        out_ref[2, :, p, :] = base - now * velocity

    for cp in sends:
        cp.wait_send()

    for cp, stays in outs:
        @pl.when(jnp.logical_not(stays))
        def _(cp=cp):
            cp.wait_send()


def fused_shards(
    image_hidden, text_hidden, modulation, text_lengths, timestep, latent,
    w_qkv, w_out, w_text_kv, norm_gain, w_up, w_down, w_head,
):
    f32, bf16 = jnp.float32, jnp.bfloat16
    rows, prompts, model = image_hidden.shape[1:]
    txt = text_hidden.shape[1]
    txt_pad = -(-txt // 16) * 16
    width = w_out.shape[0]
    units = w_up.shape[1]
    own_rows = rows * prompts
    pairs = width // 128
    vmem = pl.BlockSpec(memory_space=pltpu.VMEM)
    anym = pl.BlockSpec(memory_space=pl.ANY)
    dma = pltpu.SemaphoreType.DMA
    out = jax.ShapeDtypeStruct((3,) + latent.shape, f32)
    mods = jnp.transpose(modulation[0], (1, 0, 2))
    head = jnp.transpose(w_head)
    scratch = [
        pltpu.VMEM((rows, prompts, model), bf16),
        pltpu.VMEM((txt, model), bf16),
        pltpu.VMEM(mods.shape, f32),
        pltpu.SMEM(text_lengths.shape, jnp.int32),
        pltpu.SMEM(timestep.shape, jnp.int32),
        pltpu.VMEM(latent.shape, f32),
        pltpu.VMEM(norm_gain.shape, f32),
        pltpu.VMEM(head.shape, bf16),
        pltpu.VMEM(w_qkv.shape, bf16), pltpu.VMEM(w_out.shape, bf16), pltpu.VMEM(w_out.shape, bf16),
        pltpu.VMEM(w_text_kv.shape, bf16),
        pltpu.VMEM(w_up.shape, bf16), pltpu.VMEM(w_down.shape, bf16),
        pltpu.VMEM((model // 128, own_rows, 128), f32),
        pltpu.VMEM((prompts, rows, model), bf16),
        pltpu.VMEM((2, prompts, rows, model), bf16),
        pltpu.VMEM((2, prompts, rows, model), bf16),
        pltpu.VMEM((txt_pad, model), f32),
        pltpu.VMEM((pairs, 2, own_rows, 128), bf16),
        pltpu.VMEM((pairs, 2, own_rows, 128), bf16),
        pltpu.VMEM((pairs, 2, own_rows, 128), bf16),
        pltpu.VMEM((pairs, txt_pad, 128), bf16),
        pltpu.VMEM((pairs, txt_pad, 128), bf16),
        pltpu.VMEM((2, pairs // 2, own_rows, 256), bf16),
        pltpu.VMEM((2, pairs // 2, own_rows, 256), bf16),
        pltpu.VMEM((prompts, rows, model), f32),
        pltpu.VMEM((prompts, rows, model), f32),
        pltpu.VMEM((prompts, rows, model), bf16),
        pltpu.VMEM((own_rows, units), bf16),
        pltpu.VMEM((2, prompts, rows, model), bf16),
        pltpu.VMEM((prompts, rows, model), bf16),
        pltpu.VMEM((2, rows, model), bf16),
        pltpu.VMEM((prompts, rows, 128), f32),
        pltpu.VMEM((prompts, rows, 128), f32),
        dma((8,)), dma((10,)), dma((prompts,)), dma((prompts,)), dma((prompts,)), dma((prompts,)),
        dma((16,)), dma((16,)), dma((pairs,)), dma((pairs,)), dma((prompts // 2,)), dma((prompts // 2,)),
        dma((prompts,)), dma((prompts,)),
    ]
    stacked = pl.pallas_call(
        fused_kernel,
        out_shape=out,
        in_specs=[anym] * 13,
        out_specs=vmem,
        scratch_shapes=scratch,
        compiler_params=pltpu.CompilerParams(
            collective_id=0, has_side_effects=True, vmem_limit_bytes=60 << 20),
        name="fused_block",
    )(
        image_hidden[0], text_hidden[0], mods, text_lengths,
        timestep, latent, w_qkv, w_out, w_text_kv, norm_gain, w_up, w_down, head,
    )
    return stacked[0], stacked[1], stacked[2]


def solution(mesh):
    placed = (
        P("cfg", ("seq", "mlp"), None, None),
        P("cfg", "seq", None),
        P("cfg", None, None, None),
        P("cfg", None),
        P(),
        P(("seq", "mlp"), "cfg", None),
        P(None, None, "mlp"),
        P("mlp", None),
        P(None, None, "mlp"),
        P(),
        P(None, "mlp"),
        P("mlp", None),
        P(),
    )
    fits = mesh.shape["cfg"] == 2 and mesh.shape["seq"] == PROMPTS and mesh.shape["mlp"] == 2
    return jax.shard_map(
        fused_shards if fits else shards,
        mesh=mesh,
        in_specs=placed,
        out_specs=(
            P(("seq", "mlp"), "cfg", None),
            P(("seq", "mlp"), "cfg", None),
            P(("seq", "mlp"), "cfg", None),
        ),
        check_vma=False,
    )
```

```python
import math

import jax
import jax.numpy as jnp
from jax import lax
from jax.experimental import pallas as pl
from jax.experimental.pallas import tpu as pltpu
from jax.sharding import PartitionSpec as P

HEAD_DIM = 64
TXT = 154
STEPS = 28


EPS = 1e-06
GUIDE = 4.5
SHIFT = 3.0
PROMPTS = 8
PATCH = 64
MESH = pl.DeviceIdType.MESH


def partner_2(block, axis, stride):
    count = lax.axis_size(axis)
    route = []
    for low in range(count):
        high = low | 1 << stride
        if high != low and high < count:
            route += [(low, high), (high, low)]
    return lax.ppermute(block, axis, route)


def layer_norm(values):
    mean = jnp.mean(values, axis=-1, keepdims=True)
    centred = values - mean
    spread = jnp.mean(centred * centred, axis=-1, keepdims=True)
    return centred * lax.rsqrt(spread + EPS)


def modulate(values, shift, scale):
    return layer_norm(values) * (1.0 + scale) + shift


def head_norm(values, gain):
    shaped = values.reshape(values.shape[:-1] + (values.shape[-1] // HEAD_DIM, HEAD_DIM))
    square = jnp.mean(shaped * shaped, axis=-1, keepdims=True)
    return (shaped * lax.rsqrt(square + EPS) * gain).astype(jnp.bfloat16)


def sigma_of(index):
    level = 1.0 - index.astype(jnp.float32) / STEPS
    return SHIFT * level / (1.0 + (SHIFT - 1.0) * level)


def project_image(normed_rows, w_qkv, norm_gain):
    query = head_norm(
        jnp.einsum("tbd,de->tbe", normed_rows, w_qkv[0], preferred_element_type=jnp.float32),
        norm_gain[0],
    )
    keys = head_norm(
        jnp.einsum("tbd,de->tbe", normed_rows, w_qkv[1], preferred_element_type=jnp.float32),
        norm_gain[1],
    )
    values = jnp.einsum(
        "tbd,de->tbe", normed_rows, w_qkv[2], preferred_element_type=jnp.float32
    ).astype(jnp.bfloat16)
    flat_query = query.reshape(query.shape[:-2] + (-1,))
    flat_keys = keys.reshape(keys.shape[:-2] + (-1,))
    return jnp.concatenate([flat_query, flat_keys, values], axis=-1)


def key_terms(query, key_rows, value_rows, keep):
    factor = 1.0 / math.sqrt(HEAD_DIM)
    prompts = query.shape[1]
    if keep is None:
        keep = jnp.ones((prompts, key_rows.shape[0]), jnp.float32)

    def one_prompt(items):
        query_rows, keys_one, values_one, keep_one = items
        scores = (
            jnp.einsum("qhd,khd->hqk", query_rows, keys_one, preferred_element_type=jnp.float32)
            * factor
        )
        weights = jnp.exp(scores) * keep_one[None, None, :]
        numer = jnp.einsum(
            "hqk,khd->hqd",
            weights.astype(jnp.bfloat16),
            values_one,
            preferred_element_type=jnp.float32,
        )
        return (numer, jnp.sum(weights, axis=-1))

    return lax.map(
        one_prompt,
        (
            jnp.moveaxis(query, 1, 0),
            jnp.moveaxis(key_rows, 1, 0),
            jnp.moveaxis(value_rows, 1, 0),
            keep,
        ),
    )


def shards(
    image_hidden,
    text_hidden,
    modulation,
    text_lengths,
    timestep,
    latent,
    w_qkv,
    w_out,
    w_text_kv,
    norm_gain,
    w_up,
    w_down,
    w_head,
):
    mods = modulation[0]
    own_hidden = image_hidden[0]
    rows = own_hidden.shape[0]
    width = w_out.shape[0]
    heads = width // HEAD_DIM
    prompts = mods.shape[0]
    offset = lax.axis_index("mlp") * rows
    block_hidden = lax.all_gather(own_hidden, "mlp", axis=0, tiled=True).astype(jnp.float32)
    normed = modulate(block_hidden, mods[:, 0], mods[:, 1]).astype(jnp.bfloat16)
    projected = project_image(normed, w_qkv, norm_gain)
    block_rows = projected.shape[0]
    query = projected[..., :width].reshape(block_rows, prompts, heads, HEAD_DIM)
    own_pairs = projected[..., width:]
    text_rows = text_hidden.shape[1]
    position = lax.axis_index("seq") * text_rows + lax.iota(jnp.int32, text_rows)
    owner = position // TXT
    pick = (owner[:, None] == lax.iota(jnp.int32, prompts)[None, :]).astype(jnp.float32)
    text_shift = jnp.dot(pick, mods[:, 6], precision=lax.Precision.HIGHEST)
    text_scale = jnp.dot(pick, mods[:, 7], precision=lax.Precision.HIGHEST)
    text_normed = modulate(text_hidden[0].astype(jnp.float32), text_shift, text_scale).astype(
        jnp.bfloat16
    )
    text_keys = head_norm(
        jnp.dot(text_normed, w_text_kv[0], preferred_element_type=jnp.float32), norm_gain[2]
    )
    text_keys = text_keys.reshape(text_rows, width)
    text_values = jnp.dot(text_normed, w_text_kv[1], preferred_element_type=jnp.float32).astype(
        jnp.bfloat16
    )
    text_pairs = jnp.concatenate([text_keys, text_values], axis=-1)
    keep = (lax.iota(jnp.int32, TXT)[None, :] < text_lengths[0][:, None]).astype(jnp.float32)

    def split_pairs(pairs):
        shape = pairs.shape[:2] + (heads, HEAD_DIM)
        return (pairs[..., :width].reshape(shape), pairs[..., width:].reshape(shape))

    all_image, all_text = (
        lax.all_gather(own_pairs, "seq", axis=0, tiled=True),
        lax.all_gather(text_pairs, "seq", axis=0, tiled=True),
    )
    shaped = jnp.transpose(all_text.reshape(prompts, TXT, 2 * width), (1, 0, 2))
    key_rows, value_rows = split_pairs(shaped)
    text_numer, text_denom = key_terms(query, key_rows, value_rows, keep)
    key_rows, value_rows = split_pairs(all_image)
    image_numer, image_denom = key_terms(query, key_rows, value_rows, None)
    numer = text_numer + image_numer
    denom = text_denom + image_denom
    attended = (numer / denom[..., None]).astype(jnp.bfloat16)
    attended = jnp.transpose(attended, (2, 0, 1, 3)).reshape(block_rows, prompts, width)
    part = attended
    attention_out = lax.psum(
        jnp.einsum("tbe,ed->tbd", part, w_out, preferred_element_type=jnp.float32).astype(
            jnp.bfloat16
        ),
        "mlp",
    ).astype(jnp.float32)
    first = block_hidden + mods[:, 2] * attention_out
    mlp_in = modulate(first, mods[:, 3], mods[:, 4]).astype(jnp.bfloat16)
    raised = jnp.einsum("tbd,du->tbu", mlp_in, w_up, preferred_element_type=jnp.float32)
    activated = jax.nn.gelu(raised, approximate=True).astype(jnp.bfloat16)
    own_first = lax.dynamic_slice_in_dim(first, offset, rows, 0)
    part = activated
    mlp_out = lax.psum_scatter(
        jnp.einsum("tbu,ud->tbd", part, w_down, preferred_element_type=jnp.float32).astype(
            jnp.bfloat16
        ),
        "mlp",
        scatter_dimension=0,
        tiled=True,
    ).astype(jnp.float32)
    second = own_first + mods[:, 5] * mlp_out
    final = modulate(second, mods[:, 8], mods[:, 9]).astype(jnp.bfloat16)
    own_velocity = jnp.einsum("tbd,dp->tbp", final, w_head, preferred_element_type=jnp.float32)
    half_count = prompts // 2
    branch = lax.axis_index("cfg")
    outgoing = lax.dynamic_slice_in_dim(own_velocity, (1 - branch) * half_count, half_count, 1)
    kept = lax.dynamic_slice_in_dim(own_velocity, branch * half_count, half_count, 1)
    partner = partner_2(outgoing, "cfg", 0)
    is_conditional = branch == 0
    conditional = jnp.where(is_conditional, kept, partner)
    unconditional = jnp.where(is_conditional, partner, kept)
    velocity = unconditional + GUIDE * (conditional - unconditional)
    sigma_now = sigma_of(timestep[0])
    sigma_after = sigma_of(timestep[0] + 1)
    next_latent = latent + (sigma_after - sigma_now) * velocity
    denoised = latent - sigma_now * velocity
    return (velocity, next_latent, denoised)

def fused_kernel(
    hid_hbm, text_hbm, mod_hbm, len_hbm, step_hbm, latent_hbm, wqkv_hbm, wout_hbm, wtext_hbm,
    gain_hbm, wup_hbm, wdown_hbm, whead_hbm,
    out_ref,
    hid_ref, text_ref, mod_ref, len_ref, step_ref, latent_ref, gain_ref, whead_ref,
    wqkv, wout, wout_far, wtext, wup, wdown,
    wide, ready, gathered, normed, text_norm, q6, k6, v6, kt6, vt6, attended, att_in,
    early, proj, first_buf, mlp_in, act, down, down_in, final, half_out, half_in,
    isem, wsem, a2a_send, a2a_recv, fwd_send, fwd_recv, far_send, far_recv, at_send, at_recv,
    dn_send, dn_recv, out_send, out_recv, go_sem,
):
    c = lax.axis_index("cfg")
    s = lax.axis_index("seq")
    m = lax.axis_index("mlp")
    other = 1 - m
    ring = PROMPTS
    rows = hid_ref.shape[0]
    own_rows = rows * ring
    width = wout.shape[0]
    model = wout.shape[1]
    units = wup.shape[1]
    pairs = width // 128
    txt_pad = text_norm.shape[0]
    txt = text_ref.shape[0]
    f32, bf16 = jnp.float32, jnp.bfloat16
    partner = (c, s, other)
    sibling = (1 - c, s, m)

    bits = (lax.rem(s, 2), lax.rem(s // 2, 2), s // 4)

    def peer(k):
        return sum(((1 - bits[i]) if (k >> i) & 1 else bits[i]) * (1 << i) for i in range(3))

    inputs = []
    for i, (src, dst) in enumerate((
        (hid_hbm, hid_ref), (text_hbm, text_ref), (mod_hbm, mod_ref), (gain_hbm, gain_ref),
        (len_hbm, len_ref), (step_hbm, step_ref), (latent_hbm, latent_ref), (whead_hbm, whead_ref),
    )):
        inputs.append(pltpu.make_async_copy(src, dst, isem.at[i]))
    inputs[0].start()

    barrier = pltpu.get_barrier_semaphore()
    lead = c == 0
    tail_core = c == 1
    pl.semaphore_signal(barrier, inc=1, device_id=partner, device_id_type=MESH)

    @pl.when(lead)
    def _():
        pl.semaphore_signal(barrier, inc=1, device_id=sibling, device_id_type=MESH)

    for k in range(1, ring):
        pl.semaphore_signal(barrier, inc=1, device_id=(1, peer(k), m), device_id_type=MESH)

    for cp in inputs[1:]:
        cp.start()
    loads = []
    jobs = [(wtext_hbm.at[i], wtext.at[i]) for i in range(2)]
    jobs += [(wqkv_hbm.at[i], wqkv.at[i]) for i in range(3)]
    jobs += [(wout_hbm, wout)]
    jobs += [(wup_hbm.at[pl.ds(i * model // 2, model // 2)], wup.at[pl.ds(i * model // 2, model // 2)]) for i in range(2)]
    jobs += [(wdown_hbm.at[pl.ds(i * units // 2, units // 2)], wdown.at[pl.ds(i * units // 2, units // 2)]) for i in range(2)]
    for i, (src, dst) in enumerate(jobs):
        loads.append(pltpu.make_async_copy(src, dst, wsem.at[i]))
    for cp in loads[:2]:
        cp.start()

    inputs[0].wait()
    lanes = model // 128
    for j in range(lanes):
        tile = hid_ref[:, :, j * 128 : (j + 1) * 128]
        wide[j] = tile.astype(f32).reshape(own_rows, 128)
    for p in range(ring):
        for j in range(lanes):
            ready[p, :, j * 128 : (j + 1) * 128] = wide[j, pl.ds(p, rows, stride=ring), :].astype(bf16)
    sends = []

    def remote(src, dst, ssem, rsem, dev):
        return pltpu.make_async_remote_copy(
            src_ref=src, dst_ref=dst, send_sem=ssem, recv_sem=rsem,
            device_id=dev, device_id_type=MESH)

    def send(src, dst, ssem, rsem, dev):
        sends.append(remote(src, dst, ssem, rsem, dev))
        sends[-1].start()

    def arrive(dst, ssem, rsem, dev):
        pltpu.make_async_remote_copy(
            src_ref=dst, dst_ref=dst, send_sem=ssem, recv_sem=rsem,
            device_id=dev, device_id_type=MESH).wait_recv()

    lead_sends, tail_sends = [], []
    quarter = 4
    piece = width // (4 * quarter)

    def far_rows(core, j, i):
        q0 = (1 - bits[0]) if j & 1 else bits[0]
        q1 = (1 - bits[1]) if j & 2 else bits[1]
        start = (((q0 + 2 * q1) * 2 + core) * 2 + i) * piece
        return pl.ds(pl.multiple_of(start, 16), piece)

    near_y = (c, peer(1), m)
    near_z = (c, peer(2), m)
    near_d = (c, peer(3), m)

    def far_copy(at, i, n, dev, src=None):
        src = wout_far if src is None else src
        return remote(src.at[at], wout_far.at[at], far_send.at[i], far_recv.at[n], dev)

    def far_send_to(at, i, dev):
        sends.append(far_copy(at, i, i, dev))
        sends[-1].start()

    def far_arrive(at, i, dev):
        far_copy(at, i, i, dev).wait_recv()

    def far_cross():
        crossing = [
            far_copy(far_rows(core, 0, i), 16 * core + i, 16 * core + i, partner, wout_hbm)
            for i in range(2) for core in range(2)]
        lead_sends.extend(crossing)

        @pl.when(lead)
        def _():
            pl.semaphore_wait(barrier, 1)
            for cp in crossing:
                cp.start()

    def far_own_lead(i):
        own, near = far_rows(0, 0, i), far_rows(1, 0, i)
        first = [
            far_copy(own, 4 + i, 4 + i, near_z), far_copy(own, 2 + i, 2 + i, near_y),
            far_copy(own, 8 + i, 8 + i, sibling), far_copy(own, 6 + i, 6 + i, near_d)]
        second = far_copy(near, 18 + i, i, sibling)
        lead_sends.extend(first + [second])

        @pl.when(lead)
        def _():
            far_arrive(own, i, partner)
            for cp in first:
                cp.start()
            far_arrive(near, 16 + i, partner)
            second.start()

    def far_own_tail(i):
        own = far_rows(1, 0, i)
        copies = [
            far_copy(own, 4 + i, 4 + i, near_z), far_copy(own, 2 + i, 2 + i, near_y),
            far_copy(own, 6 + i, 6 + i, near_d)]
        tail_sends.extend(copies)

        @pl.when(tail_core)
        def _():
            far_arrive(own, i, sibling)
            for cp in copies:
                cp.start()

    def far_from_y(i):
        at = far_rows(c, 1, i)
        far_arrive(at, 2 + i, near_y)
        far_send_to(at, 10 + i, sibling)

    def far_from_z(i):
        at = far_rows(c, 2, i)
        far_arrive(at, 4 + i, near_z)
        far_send_to(at, 12 + i, sibling)

    def far_corner(i):
        at = far_rows(c, 3, i)
        far_arrive(at, 6 + i, near_d)
        far_send_to(at, 14 + i, sibling)

    def far_done():
        @pl.when(tail_core)
        def _():
            for i in range(2):
                far_arrive(far_rows(0, 0, i), 8 + i, sibling)

        for t in range(2, 8):
            far_arrive(far_rows(1 - c, t // 2, t % 2), 8 + t, sibling)

    gathered[m, s] = ready[s]
    far_cross()
    for cp in inputs[1:]:
        cp.wait()
    for cp in loads[2:5]:
        cp.start()

    def mod_row(k):
        return mod_ref[k, pl.ds(s, 1), :]

    def norm_rows(values, k):
        mean = jnp.mean(values, axis=-1, keepdims=True)
        centred = values - mean
        spread = jnp.mean(centred * centred, axis=-1, keepdims=True)
        return centred * lax.rsqrt(spread + EPS) * (1.0 + mod_row(k + 1)) + mod_row(k)

    whole_blocks = txt // 16

    def text_block(i, carry):
        at = pl.ds(pl.multiple_of(i * 16, 16), 16)
        text_norm[at, :] = norm_rows(text_ref[at, :].astype(f32), 6)
        return carry

    lax.fori_loop(0, whole_blocks, text_block, 0, unroll=3 if whole_blocks % 3 == 0 else 1)
    tail = txt - whole_blocks * 16
    if tail:
        text_norm[whole_blocks * 16 : txt, :] = norm_rows(
            text_ref[whole_blocks * 16 : txt, :].astype(f32), 6)
    if txt_pad > txt:
        text_norm[txt:txt_pad, :] = jnp.zeros((txt_pad - txt, model), f32)

    row_id = lax.broadcasted_iota(jnp.int32, (256, 256), 0)
    col_id = lax.broadcasted_iota(jnp.int32, (256, 256), 1)
    same_head = ((row_id // HEAD_DIM) == (col_id // HEAD_DIM)).astype(f32).astype(bf16)

    def square_sums(u):
        return jnp.dot((u * u).astype(bf16), same_head, preferred_element_type=f32)

    def gain_of(i):
        one = gain_ref[i : i + 1, :]
        return jnp.concatenate([one] * 4, axis=1)

    keep = (lax.broadcasted_iota(jnp.int32, (txt_pad, 128), 0) < len_ref[0, s]).astype(f32).astype(bf16)
    lane = lax.broadcasted_iota(jnp.int32, (1, 128), 1)
    low_lane = (lane < HEAD_DIM).astype(f32).astype(bf16)
    high_lane = (lane >= HEAD_DIM).astype(f32).astype(bf16)

    def project(lhs, weight, gain, mask, store):
        blocks = [
            jnp.dot(lhs, weight[:, j * 256 : (j + 1) * 256], preferred_element_type=f32)
            for j in range(width // 256)]
        if gain is not None:
            totals = [square_sums(u) for u in blocks]
            blocks = [
                u * lax.rsqrt(total * (1.0 / HEAD_DIM) + EPS) * gain
                for u, total in zip(blocks, totals)]
        for j, u in enumerate(blocks):
            for t in range(2):
                res = u[:, t * 128 : (t + 1) * 128].astype(bf16)
                store(2 * j + t, res if mask is None else res * mask)

    def to_text(buf):
        def store(i, value):
            buf[i] = value

        return store

    def to_half(buf, half):
        def store(i, value):
            buf[i, half] = value

        return store

    text_lhs = text_norm[...].astype(bf16)
    loads[0].wait()
    project(text_lhs, wtext.at[0], gain_of(2), None, to_text(kt6))
    loads[1].wait()
    project(text_lhs, wtext.at[1], None, keep, to_text(vt6))

    @pl.when(tail_core)
    def _():
        pl.semaphore_wait(barrier, 2 * ring)
        pl.semaphore_signal(go_sem, inc=1, device_id=sibling, device_id_type=MESH)

    @pl.when(lead)
    def _():
        pl.semaphore_wait(go_sem, 1)


    for k in (4, 5, 6, 7, 2, 3, 1):
        send(ready.at[peer(k)], gathered.at[m, s], a2a_send.at[k], a2a_recv.at[k], (c, peer(k), m))

    def forward(k):
        src = peer(k)
        if k:
            arrive(gathered.at[m, src], a2a_send.at[k], a2a_recv.at[k], (c, src, m))
        send(gathered.at[m, src], gathered.at[m, src], fwd_send.at[k], fwd_recv.at[k], partner)

    forward(0)
    far_own_lead(0)
    far_own_lead(1)
    for cp in loads[5:]:
        cp.start()

    def dot_t(a, b):
        return lax.dot_general(a, b, (((1,), (1,)), ((), ())), preferred_element_type=f32)

    sides = ((low_lane, high_lane), (high_lane, low_lane))

    def image_part(qh, p, half, mine, rest):
        w_img = jnp.exp(dot_t(qh, k6[p, half])).astype(bf16)
        return jnp.dot(w_img, v6[p, half] * mine + rest, preferred_element_type=f32)

    def text_part(qh, p, mine, rest):
        w_txt = jnp.exp(dot_t(qh, kt6[p])).astype(bf16)
        return jnp.dot(w_txt, vt6[p] * mine + keep * rest, preferred_element_type=f32)

    def attend_early():
        for p in range(pairs):
            q = q6[p, m]
            for n, (mine, rest) in enumerate(sides):
                qh = q * mine
                early[p, n] = image_part(qh, p, m, mine, rest) + text_part(qh, p, mine, rest)

    def attend_pair(half, p, begun):
        q = q6[p, half]
        outs = []
        for n, (mine, rest) in enumerate(sides):
            qh = q * mine
            if begun:
                outs.append(early[p, n] + image_part(qh, p, other, mine, rest))
                continue
            k = k6[p].reshape(2 * own_rows, 128)
            v = v6[p].reshape(2 * own_rows, 128)
            w_img = jnp.exp(dot_t(qh, k)).astype(bf16)
            outs.append(
                jnp.dot(w_img, v * mine + rest, preferred_element_type=f32)
                + text_part(qh, p, mine, rest))
        numer = jnp.where(lane < HEAD_DIM, outs[0], outs[1])
        denom = pltpu.roll(jnp.where(lane < HEAD_DIM, outs[1], outs[0]), HEAD_DIM, 1)
        attended[half, p // 2, :, (p % 2) * 128 : (p % 2 + 1) * 128] = (numer / denom).astype(bf16)

    def norm_blocks(half, first_at, count):
        def block(i, carry):
            normed[half, first_at + i] = norm_rows(gathered[half, first_at + i].astype(f32), 0).astype(bf16)
            return carry

        lax.fori_loop(0, count, block, 0, unroll=count)

    q_gain = gain_of(0) * (1.0 / math.sqrt(HEAD_DIM))
    k_gain = gain_of(1)

    def project_rows(half, which):
        lhs = normed[half].reshape(own_rows, model)
        buf, gain = ((q6, q_gain), (k6, k_gain), (v6, None))[which]
        project(lhs, wqkv.at[which], gain, None, to_half(buf, half))

    forward(1)
    far_own_tail(0)
    forward(2)
    far_own_tail(1)
    forward(3)
    forward(4)
    forward(5)
    forward(6)
    forward(7)
    norm_blocks(m, 0, ring)
    for i in (2, 3, 4):
        loads[i].wait()
    project_rows(m, 1)
    project_rows(m, 2)
    project_rows(m, 0)
    attend_early()

    for k in range(ring):
        src = peer(k)
        arrive(gathered.at[other, src], fwd_send.at[k], fwd_recv.at[k], partner)
    norm_blocks(other, 0, ring)
    project_rows(other, 1)
    project_rows(other, 2)
    far_from_y(0)
    far_from_z(0)
    far_from_y(1)
    far_from_z(1)

    def attend(half, base):
        for g in range(pairs // 2):
            for p in (2 * g, 2 * g + 1):
                attend_pair(half, p, base == 0)
            send(attended.at[half, g], att_in.at[half, g],
                 at_send.at[base + g], at_recv.at[base + g], partner)

    def att_arrive(half, base):
        for g in range(pairs // 2):
            arrive(att_in.at[half, g], at_send.at[base + g], at_recv.at[base + g], partner)

    attend(m, 0)
    far_corner(0)
    far_corner(1)
    project_rows(other, 0)
    attend(other, pairs // 2)
    loads[5].wait()

    def out_rows(half):
        mine = jnp.concatenate([attended[half, g] for g in range(pairs // 2)], axis=1)
        far = jnp.concatenate([att_in[half, g] for g in range(pairs // 2)], axis=1)
        for j in range(model // 512):
            cols = slice(j * 512, (j + 1) * 512)
            res = jnp.dot(mine, wout[:, cols], preferred_element_type=f32)
            res = res + jnp.dot(far, wout_far[:, cols], preferred_element_type=f32)
            proj[:, :, cols] = res.reshape(ring, rows, 512)

    def first_rows(half, hold):
        def block(i, carry):
            first = gathered[half, i].astype(f32) + mod_row(2) * proj[i]
            if hold:
                first_buf[i] = first
            mlp_in[i] = norm_rows(first, 3).astype(bf16)
            return carry

        lax.fori_loop(0, ring, block, 0, unroll=ring)

    def up():
        lhs = mlp_in[...].reshape(own_rows, model)
        for j in range(units // 512):
            cols = slice(j * 512, (j + 1) * 512)
            r = jnp.dot(lhs, wup[:, cols], preferred_element_type=f32)
            inner = math.sqrt(2.0 / math.pi) * (r + 0.044715 * (r * r * r))
            act[:, cols] = (0.5 * r * (1.0 + jnp.tanh(inner))).astype(bf16)

    def down_rows(half):
        lhs = act[...]
        for j in range(model // 512):
            cols = slice(j * 512, (j + 1) * 512)
            res = jnp.dot(lhs, wdown[:, cols], preferred_element_type=f32).astype(bf16)
            down[half, :, :, cols] = res.reshape(ring, rows, 512)

    couples = ring // 2

    def couple_at(t):
        b1 = (1 - bits[1]) if t & 1 else bits[1]
        b2 = (1 - bits[2]) if t & 2 else bits[2]
        return 2 * b1 + 4 * b2

    order = tuple(range(couples - 1, -1, -1))

    att_arrive(other, 0)
    far_done()
    out_rows(other)
    first_rows(other, False)
    for i in (6, 7):
        loads[i].wait()
    up()
    for i in (8, 9):
        loads[i].wait()
    down_rows(other)
    for t in order:
        at = pl.ds(couple_at(t), 2)
        send(down.at[other, at], down_in.at[at], dn_send.at[t], dn_recv.at[t], partner)
    att_arrive(m, pairs // 2)
    out_rows(m)
    first_rows(m, True)
    up()
    down_rows(m)

    head = whead_ref[...]
    heads2 = jnp.concatenate([head, head], axis=0)
    home = s // (ring // 2)
    slot = c * (ring // 2) + lax.rem(s, ring // 2)
    at_home = c == home
    outs = []
    for t in order:
        start = couple_at(t)
        at = pl.ds(start, 2)
        arrive(down_in.at[at], dn_send.at[t], dn_recv.at[t], partner)
        for e in range(2):
            i = start + e
            total = down[m, i].astype(f32) + down_in[i].astype(f32)
            second = first_buf[i] + mod_row(5) * total
            final[e] = norm_rows(second, 8).astype(bf16)
        hv = dot_t(final[...].reshape(2 * rows, model), heads2)
        for e in range(2):
            dest = start + e
            half_out[dest] = hv[e * rows : (e + 1) * rows]
            cp = pltpu.make_async_remote_copy(
                src_ref=half_out.at[dest], dst_ref=half_in.at[slot],
                send_sem=out_send.at[2 * t + e], recv_sem=out_recv.at[slot],
                device_id=(home, dest, m), device_id_type=MESH)
            if t:
                cp.start()
                sends.append(cp)
                continue
            stays = jnp.logical_and(at_home, s == dest)
            outs.append((cp, stays))

            @pl.when(jnp.logical_not(stays))
            def _(cp=cp):
                cp.start()

            @pl.when(stays)
            def _(dest=dest):
                half_in[slot] = half_out[dest]

    for q in range(ring):
        branch, local = q // (ring // 2), q % (ring // 2)
        prompt = c * (ring // 2) + local
        is_self = jnp.logical_and(c == branch, s == prompt)

        @pl.when(jnp.logical_not(is_self))
        def _():
            pltpu.make_async_remote_copy(
                src_ref=half_out.at[0], dst_ref=half_in.at[q],
                send_sem=out_send.at[0], recv_sem=out_recv.at[q],
                device_id=(branch, prompt, m), device_id_type=MESH).wait_recv()

    t = jnp.full((1, PATCH), step_ref[0], jnp.int32)

    def sigma(index):
        level = 1.0 - index.astype(f32) / STEPS
        return SHIFT * level / (1.0 + (SHIFT - 1.0) * level)

    now, after = sigma(t), sigma(t + 1)
    for p in range(ring // 2):
        cond = half_in[p][:, :PATCH]
        uncond = half_in[ring // 2 + p][:, :PATCH]
        velocity = uncond + GUIDE * (cond - uncond)
        base = latent_ref[:, p, :]
        out_ref[0, :, p, :] = velocity
        out_ref[1, :, p, :] = base + (after - now) * velocity
        out_ref[2, :, p, :] = base - now * velocity

    for cp in sends:
        cp.wait_send()

    @pl.when(lead)
    def _():
        for cp in lead_sends:
            cp.wait_send()

    @pl.when(tail_core)
    def _():
        for cp in tail_sends:
            cp.wait_send()

    for cp, stays in outs:
        @pl.when(jnp.logical_not(stays))
        def _(cp=cp):
            cp.wait_send()


def fused_shards(
    image_hidden, text_hidden, modulation, text_lengths, timestep, latent,
    w_qkv, w_out, w_text_kv, norm_gain, w_up, w_down, w_head,
):
    f32, bf16 = jnp.float32, jnp.bfloat16
    rows, prompts, model = image_hidden.shape[1:]
    txt = text_hidden.shape[1]
    txt_pad = -(-txt // 16) * 16
    width = w_out.shape[0]
    units = w_up.shape[1]
    own_rows = rows * prompts
    pairs = width // 128
    vmem = pl.BlockSpec(memory_space=pltpu.VMEM)
    anym = pl.BlockSpec(memory_space=pl.ANY)
    dma = pltpu.SemaphoreType.DMA
    out = jax.ShapeDtypeStruct((3,) + latent.shape, f32)
    mods = jnp.transpose(modulation[0], (1, 0, 2))
    head = jnp.transpose(w_head)
    scratch = [
        pltpu.VMEM((rows, prompts, model), bf16),
        pltpu.VMEM((txt, model), bf16),
        pltpu.VMEM(mods.shape, f32),
        pltpu.SMEM(text_lengths.shape, jnp.int32),
        pltpu.SMEM(timestep.shape, jnp.int32),
        pltpu.VMEM(latent.shape, f32),
        pltpu.VMEM(norm_gain.shape, f32),
        pltpu.VMEM(head.shape, bf16),
        pltpu.VMEM(w_qkv.shape, bf16), pltpu.VMEM(w_out.shape, bf16), pltpu.VMEM(w_out.shape, bf16),
        pltpu.VMEM(w_text_kv.shape, bf16),
        pltpu.VMEM(w_up.shape, bf16), pltpu.VMEM(w_down.shape, bf16),
        pltpu.VMEM((model // 128, own_rows, 128), f32),
        pltpu.VMEM((prompts, rows, model), bf16),
        pltpu.VMEM((2, prompts, rows, model), bf16),
        pltpu.VMEM((2, prompts, rows, model), bf16),
        pltpu.VMEM((txt_pad, model), f32),
        pltpu.VMEM((pairs, 2, own_rows, 128), bf16),
        pltpu.VMEM((pairs, 2, own_rows, 128), bf16),
        pltpu.VMEM((pairs, 2, own_rows, 128), bf16),
        pltpu.VMEM((pairs, txt_pad, 128), bf16),
        pltpu.VMEM((pairs, txt_pad, 128), bf16),
        pltpu.VMEM((2, pairs // 2, own_rows, 256), bf16),
        pltpu.VMEM((2, pairs // 2, own_rows, 256), bf16),
        pltpu.VMEM((pairs, 2, own_rows, 128), f32),
        pltpu.VMEM((prompts, rows, model), f32),
        pltpu.VMEM((prompts, rows, model), f32),
        pltpu.VMEM((prompts, rows, model), bf16),
        pltpu.VMEM((own_rows, units), bf16),
        pltpu.VMEM((2, prompts, rows, model), bf16),
        pltpu.VMEM((prompts, rows, model), bf16),
        pltpu.VMEM((2, rows, model), bf16),
        pltpu.VMEM((prompts, rows, 128), f32),
        pltpu.VMEM((prompts, rows, 128), f32),
        dma((8,)), dma((10,)), dma((prompts,)), dma((prompts,)), dma((prompts,)), dma((prompts,)),
        dma((20,)), dma((20,)), dma((pairs,)), dma((pairs,)), dma((prompts // 2,)), dma((prompts // 2,)),
        dma((prompts,)), dma((prompts,)), pltpu.SemaphoreType.REGULAR,
    ]
    stacked = pl.pallas_call(
        fused_kernel,
        out_shape=out,
        in_specs=[anym] * 13,
        out_specs=vmem,
        scratch_shapes=scratch,
        compiler_params=pltpu.CompilerParams(
            collective_id=0, has_side_effects=True, vmem_limit_bytes=60 << 20),
        name="fused_block",
    )(
        image_hidden[0], text_hidden[0], mods, text_lengths,
        timestep, latent, w_qkv, w_out, w_text_kv, norm_gain, w_up, w_down, head,
    )
    return stacked[0], stacked[1], stacked[2]


def solution(mesh):
    placed = (
        P("cfg", ("seq", "mlp"), None, None),
        P("cfg", "seq", None),
        P("cfg", None, None, None),
        P("cfg", None),
        P(),
        P(("seq", "mlp"), "cfg", None),
        P(None, None, "mlp"),
        P("mlp", None),
        P(None, None, "mlp"),
        P(),
        P(None, "mlp"),
        P("mlp", None),
        P(),
    )
    fits = mesh.shape["cfg"] == 2 and mesh.shape["seq"] == PROMPTS and mesh.shape["mlp"] == 2
    return jax.shard_map(
        fused_shards if fits else shards,
        mesh=mesh,
        in_specs=placed,
        out_specs=(
            P(("seq", "mlp"), "cfg", None),
            P(("seq", "mlp"), "cfg", None),
            P(("seq", "mlp"), "cfg", None),
        ),
        check_vma=False,
    )
```

```python
import math

import jax
import jax.numpy as jnp
from jax import lax
from jax.experimental import pallas as pl
from jax.experimental.pallas import tpu as pltpu
from jax.sharding import PartitionSpec as P

HEAD_DIM = 64
TXT = 154
STEPS = 28


EPS = 1e-06
GUIDE = 4.5
SHIFT = 3.0
PROMPTS = 8
PATCH = 64
MESH = pl.DeviceIdType.MESH


def partner_2(block, axis, stride):
    count = lax.axis_size(axis)
    route = []
    for low in range(count):
        high = low | 1 << stride
        if high != low and high < count:
            route += [(low, high), (high, low)]
    return lax.ppermute(block, axis, route)


def layer_norm(values):
    mean = jnp.mean(values, axis=-1, keepdims=True)
    centred = values - mean
    spread = jnp.mean(centred * centred, axis=-1, keepdims=True)
    return centred * lax.rsqrt(spread + EPS)


def modulate(values, shift, scale):
    return layer_norm(values) * (1.0 + scale) + shift


def head_norm(values, gain):
    shaped = values.reshape(values.shape[:-1] + (values.shape[-1] // HEAD_DIM, HEAD_DIM))
    square = jnp.mean(shaped * shaped, axis=-1, keepdims=True)
    return (shaped * lax.rsqrt(square + EPS) * gain).astype(jnp.bfloat16)


def sigma_of(index):
    level = 1.0 - index.astype(jnp.float32) / STEPS
    return SHIFT * level / (1.0 + (SHIFT - 1.0) * level)


def project_image(normed_rows, w_qkv, norm_gain):
    query = head_norm(
        jnp.einsum("tbd,de->tbe", normed_rows, w_qkv[0], preferred_element_type=jnp.float32),
        norm_gain[0],
    )
    keys = head_norm(
        jnp.einsum("tbd,de->tbe", normed_rows, w_qkv[1], preferred_element_type=jnp.float32),
        norm_gain[1],
    )
    values = jnp.einsum(
        "tbd,de->tbe", normed_rows, w_qkv[2], preferred_element_type=jnp.float32
    ).astype(jnp.bfloat16)
    flat_query = query.reshape(query.shape[:-2] + (-1,))
    flat_keys = keys.reshape(keys.shape[:-2] + (-1,))
    return jnp.concatenate([flat_query, flat_keys, values], axis=-1)


def key_terms(query, key_rows, value_rows, keep):
    factor = 1.0 / math.sqrt(HEAD_DIM)
    prompts = query.shape[1]
    if keep is None:
        keep = jnp.ones((prompts, key_rows.shape[0]), jnp.float32)

    def one_prompt(items):
        query_rows, keys_one, values_one, keep_one = items
        scores = (
            jnp.einsum("qhd,khd->hqk", query_rows, keys_one, preferred_element_type=jnp.float32)
            * factor
        )
        weights = jnp.exp(scores) * keep_one[None, None, :]
        numer = jnp.einsum(
            "hqk,khd->hqd",
            weights.astype(jnp.bfloat16),
            values_one,
            preferred_element_type=jnp.float32,
        )
        return (numer, jnp.sum(weights, axis=-1))

    return lax.map(
        one_prompt,
        (
            jnp.moveaxis(query, 1, 0),
            jnp.moveaxis(key_rows, 1, 0),
            jnp.moveaxis(value_rows, 1, 0),
            keep,
        ),
    )


def shards(
    image_hidden,
    text_hidden,
    modulation,
    text_lengths,
    timestep,
    latent,
    w_qkv,
    w_out,
    w_text_kv,
    norm_gain,
    w_up,
    w_down,
    w_head,
):
    mods = modulation[0]
    own_hidden = image_hidden[0]
    rows = own_hidden.shape[0]
    width = w_out.shape[0]
    heads = width // HEAD_DIM
    prompts = mods.shape[0]
    offset = lax.axis_index("mlp") * rows
    block_hidden = lax.all_gather(own_hidden, "mlp", axis=0, tiled=True).astype(jnp.float32)
    normed = modulate(block_hidden, mods[:, 0], mods[:, 1]).astype(jnp.bfloat16)
    projected = project_image(normed, w_qkv, norm_gain)
    block_rows = projected.shape[0]
    query = projected[..., :width].reshape(block_rows, prompts, heads, HEAD_DIM)
    own_pairs = projected[..., width:]
    text_rows = text_hidden.shape[1]
    position = lax.axis_index("seq") * text_rows + lax.iota(jnp.int32, text_rows)
    owner = position // TXT
    pick = (owner[:, None] == lax.iota(jnp.int32, prompts)[None, :]).astype(jnp.float32)
    text_shift = jnp.dot(pick, mods[:, 6], precision=lax.Precision.HIGHEST)
    text_scale = jnp.dot(pick, mods[:, 7], precision=lax.Precision.HIGHEST)
    text_normed = modulate(text_hidden[0].astype(jnp.float32), text_shift, text_scale).astype(
        jnp.bfloat16
    )
    text_keys = head_norm(
        jnp.dot(text_normed, w_text_kv[0], preferred_element_type=jnp.float32), norm_gain[2]
    )
    text_keys = text_keys.reshape(text_rows, width)
    text_values = jnp.dot(text_normed, w_text_kv[1], preferred_element_type=jnp.float32).astype(
        jnp.bfloat16
    )
    text_pairs = jnp.concatenate([text_keys, text_values], axis=-1)
    keep = (lax.iota(jnp.int32, TXT)[None, :] < text_lengths[0][:, None]).astype(jnp.float32)

    def split_pairs(pairs):
        shape = pairs.shape[:2] + (heads, HEAD_DIM)
        return (pairs[..., :width].reshape(shape), pairs[..., width:].reshape(shape))

    all_image, all_text = (
        lax.all_gather(own_pairs, "seq", axis=0, tiled=True),
        lax.all_gather(text_pairs, "seq", axis=0, tiled=True),
    )
    shaped = jnp.transpose(all_text.reshape(prompts, TXT, 2 * width), (1, 0, 2))
    key_rows, value_rows = split_pairs(shaped)
    text_numer, text_denom = key_terms(query, key_rows, value_rows, keep)
    key_rows, value_rows = split_pairs(all_image)
    image_numer, image_denom = key_terms(query, key_rows, value_rows, None)
    numer = text_numer + image_numer
    denom = text_denom + image_denom
    attended = (numer / denom[..., None]).astype(jnp.bfloat16)
    attended = jnp.transpose(attended, (2, 0, 1, 3)).reshape(block_rows, prompts, width)
    part = attended
    attention_out = lax.psum(
        jnp.einsum("tbe,ed->tbd", part, w_out, preferred_element_type=jnp.float32).astype(
            jnp.bfloat16
        ),
        "mlp",
    ).astype(jnp.float32)
    first = block_hidden + mods[:, 2] * attention_out
    mlp_in = modulate(first, mods[:, 3], mods[:, 4]).astype(jnp.bfloat16)
    raised = jnp.einsum("tbd,du->tbu", mlp_in, w_up, preferred_element_type=jnp.float32)
    activated = jax.nn.gelu(raised, approximate=True).astype(jnp.bfloat16)
    own_first = lax.dynamic_slice_in_dim(first, offset, rows, 0)
    part = activated
    mlp_out = lax.psum_scatter(
        jnp.einsum("tbu,ud->tbd", part, w_down, preferred_element_type=jnp.float32).astype(
            jnp.bfloat16
        ),
        "mlp",
        scatter_dimension=0,
        tiled=True,
    ).astype(jnp.float32)
    second = own_first + mods[:, 5] * mlp_out
    final = modulate(second, mods[:, 8], mods[:, 9]).astype(jnp.bfloat16)
    own_velocity = jnp.einsum("tbd,dp->tbp", final, w_head, preferred_element_type=jnp.float32)
    half_count = prompts // 2
    branch = lax.axis_index("cfg")
    outgoing = lax.dynamic_slice_in_dim(own_velocity, (1 - branch) * half_count, half_count, 1)
    kept = lax.dynamic_slice_in_dim(own_velocity, branch * half_count, half_count, 1)
    partner = partner_2(outgoing, "cfg", 0)
    is_conditional = branch == 0
    conditional = jnp.where(is_conditional, kept, partner)
    unconditional = jnp.where(is_conditional, partner, kept)
    velocity = unconditional + GUIDE * (conditional - unconditional)
    sigma_now = sigma_of(timestep[0])
    sigma_after = sigma_of(timestep[0] + 1)
    next_latent = latent + (sigma_after - sigma_now) * velocity
    denoised = latent - sigma_now * velocity
    return (velocity, next_latent, denoised)

def fused_kernel(
    hid_hbm, text_hbm, mod_hbm, len_hbm, step_hbm, latent_hbm, wqkv_hbm, wout_hbm, wtext_hbm,
    gain_hbm, wup_hbm, wdown_hbm, whead_hbm,
    out_ref,
    hid_ref, text_ref, mod_ref, len_ref, step_ref, latent_ref, gain_ref, whead_ref,
    wqkv, wout, wout_far, wtext, wup, wdown,
    wide, ready, gathered, normed, text_norm, q6, k6, v6, kt6, vt6, attended, att_in,
    early, proj, first_buf, mlp_in, act, down, down_in, final, half_out, half_in,
    isem, wsem, a2a_send, a2a_recv, fwd_send, fwd_recv, far_send, far_recv, at_send, at_recv,
    dn_send, dn_recv, out_send, out_recv, go_sem,
):
    c = lax.axis_index("cfg")
    s = lax.axis_index("seq")
    m = lax.axis_index("mlp")
    other = 1 - m
    ring = PROMPTS
    rows = hid_ref.shape[0]
    own_rows = rows * ring
    width = wout.shape[0]
    model = wout.shape[1]
    units = wup.shape[1]
    pairs = width // 128
    txt_pad = text_norm.shape[0]
    txt = text_ref.shape[0]
    f32, bf16 = jnp.float32, jnp.bfloat16
    partner = (c, s, other)
    sibling = (1 - c, s, m)

    bits = (lax.rem(s, 2), lax.rem(s // 2, 2), s // 4)

    def peer(k):
        return sum(((1 - bits[i]) if (k >> i) & 1 else bits[i]) * (1 << i) for i in range(3))

    inputs = []
    for i, (src, dst) in enumerate((
        (hid_hbm, hid_ref), (text_hbm, text_ref), (mod_hbm, mod_ref), (gain_hbm, gain_ref),
        (len_hbm, len_ref), (step_hbm, step_ref), (latent_hbm, latent_ref), (whead_hbm, whead_ref),
    )):
        inputs.append(pltpu.make_async_copy(src, dst, isem.at[i]))
    inputs[0].start()

    barrier = pltpu.get_barrier_semaphore()
    lead = c == 0
    tail_core = c == 1
    pl.semaphore_signal(barrier, inc=1, device_id=partner, device_id_type=MESH)

    @pl.when(lead)
    def _():
        pl.semaphore_signal(barrier, inc=1, device_id=sibling, device_id_type=MESH)

    for k in range(1, ring):
        pl.semaphore_signal(barrier, inc=1, device_id=(1, peer(k), m), device_id_type=MESH)

    for cp in inputs[1:]:
        cp.start()
    loads = []
    jobs = [(wtext_hbm.at[i], wtext.at[i]) for i in range(2)]
    jobs += [(wqkv_hbm.at[i], wqkv.at[i]) for i in range(3)]
    jobs += [(wout_hbm, wout)]
    jobs += [(wup_hbm.at[pl.ds(i * model // 2, model // 2)], wup.at[pl.ds(i * model // 2, model // 2)]) for i in range(2)]
    jobs += [(wdown_hbm.at[pl.ds(i * units // 2, units // 2)], wdown.at[pl.ds(i * units // 2, units // 2)]) for i in range(2)]
    for i, (src, dst) in enumerate(jobs):
        loads.append(pltpu.make_async_copy(src, dst, wsem.at[i]))
    for cp in loads[:2]:
        cp.start()

    inputs[0].wait()
    lanes = model // 128
    for j in range(lanes):
        tile = hid_ref[:, :, j * 128 : (j + 1) * 128]
        wide[j] = tile.astype(f32).reshape(own_rows, 128)
    for p in range(ring):
        for j in range(lanes):
            ready[p, :, j * 128 : (j + 1) * 128] = wide[j, pl.ds(p, rows, stride=ring), :].astype(bf16)
    sends = []

    def remote(src, dst, ssem, rsem, dev):
        return pltpu.make_async_remote_copy(
            src_ref=src, dst_ref=dst, send_sem=ssem, recv_sem=rsem,
            device_id=dev, device_id_type=MESH)

    def send(src, dst, ssem, rsem, dev):
        sends.append(remote(src, dst, ssem, rsem, dev))
        sends[-1].start()

    def arrive(dst, ssem, rsem, dev):
        pltpu.make_async_remote_copy(
            src_ref=dst, dst_ref=dst, send_sem=ssem, recv_sem=rsem,
            device_id=dev, device_id_type=MESH).wait_recv()

    lead_sends, tail_sends = [], []
    quarter = 4
    piece = width // (4 * quarter)

    def far_rows(core, j, i):
        q0 = (1 - bits[0]) if j & 1 else bits[0]
        q1 = (1 - bits[1]) if j & 2 else bits[1]
        start = (((q0 + 2 * q1) * 2 + core) * 2 + i) * piece
        return pl.ds(pl.multiple_of(start, 16), piece)

    near_y = (c, peer(1), m)
    near_z = (c, peer(2), m)

    def far_copy(at, i, n, dev, src=None):
        src = wout_far if src is None else src
        return remote(src.at[at], wout_far.at[at], far_send.at[i], far_recv.at[n], dev)

    def far_send_to(at, i, dev):
        sends.append(far_copy(at, i, i, dev))
        sends[-1].start()

    def far_arrive(at, i, dev):
        far_copy(at, i, i, dev).wait_recv()

    def far_cross():
        crossing = [
            far_copy(far_rows(core, 0, i), 16 * core + i, 16 * core + i, partner, wout_hbm)
            for i in range(2) for core in range(2)]
        lead_sends.extend(crossing)

        @pl.when(lead)
        def _():
            pl.semaphore_wait(barrier, 1)
            for cp in crossing:
                cp.start()

    def far_own_lead(i):
        own, near = far_rows(0, 0, i), far_rows(1, 0, i)
        first = [
            far_copy(own, 4 + i, 4 + i, near_z), far_copy(own, 2 + i, 2 + i, near_y),
            far_copy(own, 8 + i, 8 + i, sibling)]
        second = far_copy(near, 18 + i, i, sibling)
        lead_sends.extend(first + [second])

        @pl.when(lead)
        def _():
            far_arrive(own, i, partner)
            for cp in first:
                cp.start()
            far_arrive(near, 16 + i, partner)
            second.start()

    def far_own_tail(i):
        own = far_rows(1, 0, i)
        copies = [far_copy(own, 4 + i, 4 + i, near_z), far_copy(own, 2 + i, 2 + i, near_y)]
        tail_sends.extend(copies)

        @pl.when(tail_core)
        def _():
            far_arrive(own, i, sibling)
            for cp in copies:
                cp.start()

    def far_from_y(i):
        at = far_rows(c, 1, i)
        far_arrive(at, 2 + i, near_y)
        if i == 0:
            far_send_to(at, 6, near_z)
        far_send_to(at, 10 + i, sibling)

    def far_from_z(i):
        at = far_rows(c, 2, i)
        far_arrive(at, 4 + i, near_z)
        if i == 1:
            far_send_to(at, 7, near_y)
        far_send_to(at, 12 + i, sibling)

    def far_corner(i):
        at = far_rows(c, 3, i)
        far_arrive(at, 6 + i, near_z if i == 0 else near_y)
        far_send_to(at, 14 + i, sibling)

    def far_done():
        @pl.when(tail_core)
        def _():
            for i in range(2):
                far_arrive(far_rows(0, 0, i), 8 + i, sibling)

        for t in range(2, 8):
            far_arrive(far_rows(1 - c, t // 2, t % 2), 8 + t, sibling)

    gathered[m, s] = ready[s]
    far_cross()
    for cp in inputs[1:]:
        cp.wait()
    for cp in loads[2:5]:
        cp.start()

    def mod_row(k):
        return mod_ref[k, pl.ds(s, 1), :]

    def norm_rows(values, k):
        mean = jnp.mean(values, axis=-1, keepdims=True)
        centred = values - mean
        spread = jnp.mean(centred * centred, axis=-1, keepdims=True)
        return centred * lax.rsqrt(spread + EPS) * (1.0 + mod_row(k + 1)) + mod_row(k)

    whole_blocks = txt // 16

    def text_block(i, carry):
        at = pl.ds(pl.multiple_of(i * 16, 16), 16)
        text_norm[at, :] = norm_rows(text_ref[at, :].astype(f32), 6)
        return carry

    lax.fori_loop(0, whole_blocks, text_block, 0, unroll=3 if whole_blocks % 3 == 0 else 1)
    tail = txt - whole_blocks * 16
    if tail:
        text_norm[whole_blocks * 16 : txt, :] = norm_rows(
            text_ref[whole_blocks * 16 : txt, :].astype(f32), 6)
    if txt_pad > txt:
        text_norm[txt:txt_pad, :] = jnp.zeros((txt_pad - txt, model), f32)

    row_id = lax.broadcasted_iota(jnp.int32, (256, 256), 0)
    col_id = lax.broadcasted_iota(jnp.int32, (256, 256), 1)
    same_head = ((row_id // HEAD_DIM) == (col_id // HEAD_DIM)).astype(f32).astype(bf16)

    def square_sums(u):
        return jnp.dot((u * u).astype(bf16), same_head, preferred_element_type=f32)

    def gain_of(i):
        one = gain_ref[i : i + 1, :]
        return jnp.concatenate([one] * 4, axis=1)

    keep = (lax.broadcasted_iota(jnp.int32, (txt_pad, 128), 0) < len_ref[0, s]).astype(f32).astype(bf16)
    lane = lax.broadcasted_iota(jnp.int32, (1, 128), 1)
    low_lane = (lane < HEAD_DIM).astype(f32).astype(bf16)
    high_lane = (lane >= HEAD_DIM).astype(f32).astype(bf16)

    def project(lhs, weight, gain, mask, store):
        blocks = [
            jnp.dot(lhs, weight[:, j * 256 : (j + 1) * 256], preferred_element_type=f32)
            for j in range(width // 256)]
        if gain is not None:
            totals = [square_sums(u) for u in blocks]
            blocks = [
                u * lax.rsqrt(total * (1.0 / HEAD_DIM) + EPS) * gain
                for u, total in zip(blocks, totals)]
        for j, u in enumerate(blocks):
            for t in range(2):
                res = u[:, t * 128 : (t + 1) * 128].astype(bf16)
                store(2 * j + t, res if mask is None else res * mask)

    def to_text(buf):
        def store(i, value):
            buf[i] = value

        return store

    def to_half(buf, half):
        def store(i, value):
            buf[i, half] = value

        return store

    text_lhs = text_norm[...].astype(bf16)
    loads[0].wait()
    project(text_lhs, wtext.at[0], gain_of(2), None, to_text(kt6))
    loads[1].wait()
    project(text_lhs, wtext.at[1], None, keep, to_text(vt6))

    @pl.when(tail_core)
    def _():
        pl.semaphore_wait(barrier, 2 * ring)
        pl.semaphore_signal(go_sem, inc=1, device_id=sibling, device_id_type=MESH)

    @pl.when(lead)
    def _():
        pl.semaphore_wait(go_sem, 1)


    for k in (4, 5, 6, 7, 2, 3, 1):
        send(ready.at[peer(k)], gathered.at[m, s], a2a_send.at[k], a2a_recv.at[k], (c, peer(k), m))

    def forward(k):
        src = peer(k)
        if k:
            arrive(gathered.at[m, src], a2a_send.at[k], a2a_recv.at[k], (c, src, m))
        send(gathered.at[m, src], gathered.at[m, src], fwd_send.at[k], fwd_recv.at[k], partner)

    forward(0)
    for cp in loads[5:]:
        cp.start()

    def dot_t(a, b):
        return lax.dot_general(a, b, (((1,), (1,)), ((), ())), preferred_element_type=f32)

    sides = ((low_lane, high_lane), (high_lane, low_lane))

    def image_part(qh, p, half, mine, rest):
        w_img = jnp.exp(dot_t(qh, k6[p, half])).astype(bf16)
        return jnp.dot(w_img, v6[p, half] * mine + rest, preferred_element_type=f32)

    def text_part(qh, p, mine, rest):
        w_txt = jnp.exp(dot_t(qh, kt6[p])).astype(bf16)
        return jnp.dot(w_txt, vt6[p] * mine + keep * rest, preferred_element_type=f32)

    def attend_early():
        for p in range(pairs):
            q = q6[p, m]
            for n, (mine, rest) in enumerate(sides):
                qh = q * mine
                early[p, n] = image_part(qh, p, m, mine, rest) + text_part(qh, p, mine, rest)

    def attend_pair(half, p, begun):
        q = q6[p, half]
        outs = []
        for n, (mine, rest) in enumerate(sides):
            qh = q * mine
            if begun:
                outs.append(early[p, n] + image_part(qh, p, other, mine, rest))
                continue
            k = k6[p].reshape(2 * own_rows, 128)
            v = v6[p].reshape(2 * own_rows, 128)
            w_img = jnp.exp(dot_t(qh, k)).astype(bf16)
            outs.append(
                jnp.dot(w_img, v * mine + rest, preferred_element_type=f32)
                + text_part(qh, p, mine, rest))
        numer = jnp.where(lane < HEAD_DIM, outs[0], outs[1])
        denom = pltpu.roll(jnp.where(lane < HEAD_DIM, outs[1], outs[0]), HEAD_DIM, 1)
        attended[half, p // 2, :, (p % 2) * 128 : (p % 2 + 1) * 128] = (numer / denom).astype(bf16)

    def norm_blocks(half, first_at, count):
        def block(i, carry):
            normed[half, first_at + i] = norm_rows(gathered[half, first_at + i].astype(f32), 0).astype(bf16)
            return carry

        lax.fori_loop(0, count, block, 0, unroll=count)

    q_gain = gain_of(0) * (1.0 / math.sqrt(HEAD_DIM))
    k_gain = gain_of(1)

    def project_rows(half, which):
        lhs = normed[half].reshape(own_rows, model)
        buf, gain = ((q6, q_gain), (k6, k_gain), (v6, None))[which]
        project(lhs, wqkv.at[which], gain, None, to_half(buf, half))

    forward(1)
    far_own_lead(0)
    far_own_lead(1)
    forward(2)
    far_own_tail(0)
    forward(3)
    forward(4)
    far_own_tail(1)
    forward(5)
    forward(6)
    forward(7)
    norm_blocks(m, 0, ring)
    for i in (2, 3, 4):
        loads[i].wait()
    project_rows(m, 1)
    project_rows(m, 2)
    project_rows(m, 0)
    attend_early()
    far_from_y(0)
    far_from_z(0)

    for k in range(ring):
        src = peer(k)
        arrive(gathered.at[other, src], fwd_send.at[k], fwd_recv.at[k], partner)
    norm_blocks(other, 0, ring)
    project_rows(other, 1)
    project_rows(other, 2)
    far_from_y(1)
    far_from_z(1)

    def attend(half, base):
        for g in range(pairs // 2):
            for p in (2 * g, 2 * g + 1):
                attend_pair(half, p, base == 0)
            send(attended.at[half, g], att_in.at[half, g],
                 at_send.at[base + g], at_recv.at[base + g], partner)

    def att_arrive(half, base):
        for g in range(pairs // 2):
            arrive(att_in.at[half, g], at_send.at[base + g], at_recv.at[base + g], partner)

    attend(m, 0)
    far_corner(0)
    project_rows(other, 0)
    far_corner(1)
    attend(other, pairs // 2)
    loads[5].wait()

    def out_rows(half):
        mine = jnp.concatenate([attended[half, g] for g in range(pairs // 2)], axis=1)
        far = jnp.concatenate([att_in[half, g] for g in range(pairs // 2)], axis=1)
        for j in range(model // 512):
            cols = slice(j * 512, (j + 1) * 512)
            res = jnp.dot(mine, wout[:, cols], preferred_element_type=f32)
            res = res + jnp.dot(far, wout_far[:, cols], preferred_element_type=f32)
            proj[:, :, cols] = res.reshape(ring, rows, 512)

    def first_rows(half, hold):
        def block(i, carry):
            first = gathered[half, i].astype(f32) + mod_row(2) * proj[i]
            if hold:
                first_buf[i] = first
            mlp_in[i] = norm_rows(first, 3).astype(bf16)
            return carry

        lax.fori_loop(0, ring, block, 0, unroll=ring)

    def up():
        lhs = mlp_in[...].reshape(own_rows, model)
        for j in range(units // 512):
            cols = slice(j * 512, (j + 1) * 512)
            r = jnp.dot(lhs, wup[:, cols], preferred_element_type=f32)
            inner = math.sqrt(2.0 / math.pi) * (r + 0.044715 * (r * r * r))
            act[:, cols] = (0.5 * r * (1.0 + jnp.tanh(inner))).astype(bf16)

    def down_rows(half):
        lhs = act[...]
        for j in range(model // 512):
            cols = slice(j * 512, (j + 1) * 512)
            res = jnp.dot(lhs, wdown[:, cols], preferred_element_type=f32).astype(bf16)
            down[half, :, :, cols] = res.reshape(ring, rows, 512)

    couples = ring // 2

    def couple_at(t):
        b1 = (1 - bits[1]) if t & 1 else bits[1]
        b2 = (1 - bits[2]) if t & 2 else bits[2]
        return 2 * b1 + 4 * b2

    order = tuple(range(couples - 1, -1, -1))

    att_arrive(other, 0)
    far_done()
    out_rows(other)
    first_rows(other, False)
    for i in (6, 7):
        loads[i].wait()
    up()
    for i in (8, 9):
        loads[i].wait()
    down_rows(other)
    for t in order:
        at = pl.ds(couple_at(t), 2)
        send(down.at[other, at], down_in.at[at], dn_send.at[t], dn_recv.at[t], partner)
    att_arrive(m, pairs // 2)
    out_rows(m)
    first_rows(m, True)
    up()
    down_rows(m)

    head = whead_ref[...]
    heads2 = jnp.concatenate([head, head], axis=0)
    home = s // (ring // 2)
    slot = c * (ring // 2) + lax.rem(s, ring // 2)
    at_home = c == home
    outs = []
    for t in order:
        start = couple_at(t)
        at = pl.ds(start, 2)
        arrive(down_in.at[at], dn_send.at[t], dn_recv.at[t], partner)
        for e in range(2):
            i = start + e
            total = down[m, i].astype(f32) + down_in[i].astype(f32)
            second = first_buf[i] + mod_row(5) * total
            final[e] = norm_rows(second, 8).astype(bf16)
        hv = dot_t(final[...].reshape(2 * rows, model), heads2)
        for e in range(2):
            dest = start + e
            half_out[dest] = hv[e * rows : (e + 1) * rows]
            cp = pltpu.make_async_remote_copy(
                src_ref=half_out.at[dest], dst_ref=half_in.at[slot],
                send_sem=out_send.at[2 * t + e], recv_sem=out_recv.at[slot],
                device_id=(home, dest, m), device_id_type=MESH)
            if t:
                cp.start()
                sends.append(cp)
                continue
            stays = jnp.logical_and(at_home, s == dest)
            outs.append((cp, stays))

            @pl.when(jnp.logical_not(stays))
            def _(cp=cp):
                cp.start()

            @pl.when(stays)
            def _(dest=dest):
                half_in[slot] = half_out[dest]

    for q in range(ring):
        branch, local = q // (ring // 2), q % (ring // 2)
        prompt = c * (ring // 2) + local
        is_self = jnp.logical_and(c == branch, s == prompt)

        @pl.when(jnp.logical_not(is_self))
        def _():
            pltpu.make_async_remote_copy(
                src_ref=half_out.at[0], dst_ref=half_in.at[q],
                send_sem=out_send.at[0], recv_sem=out_recv.at[q],
                device_id=(branch, prompt, m), device_id_type=MESH).wait_recv()

    t = jnp.full((1, PATCH), step_ref[0], jnp.int32)

    def sigma(index):
        level = 1.0 - index.astype(f32) / STEPS
        return SHIFT * level / (1.0 + (SHIFT - 1.0) * level)

    now, after = sigma(t), sigma(t + 1)
    for p in range(ring // 2):
        cond = half_in[p][:, :PATCH]
        uncond = half_in[ring // 2 + p][:, :PATCH]
        velocity = uncond + GUIDE * (cond - uncond)
        base = latent_ref[:, p, :]
        out_ref[0, :, p, :] = velocity
        out_ref[1, :, p, :] = base + (after - now) * velocity
        out_ref[2, :, p, :] = base - now * velocity

    for cp in sends:
        cp.wait_send()

    @pl.when(lead)
    def _():
        for cp in lead_sends:
            cp.wait_send()

    @pl.when(tail_core)
    def _():
        for cp in tail_sends:
            cp.wait_send()

    for cp, stays in outs:
        @pl.when(jnp.logical_not(stays))
        def _(cp=cp):
            cp.wait_send()


def fused_shards(
    image_hidden, text_hidden, modulation, text_lengths, timestep, latent,
    w_qkv, w_out, w_text_kv, norm_gain, w_up, w_down, w_head,
):
    f32, bf16 = jnp.float32, jnp.bfloat16
    rows, prompts, model = image_hidden.shape[1:]
    txt = text_hidden.shape[1]
    txt_pad = -(-txt // 16) * 16
    width = w_out.shape[0]
    units = w_up.shape[1]
    own_rows = rows * prompts
    pairs = width // 128
    vmem = pl.BlockSpec(memory_space=pltpu.VMEM)
    anym = pl.BlockSpec(memory_space=pl.ANY)
    dma = pltpu.SemaphoreType.DMA
    out = jax.ShapeDtypeStruct((3,) + latent.shape, f32)
    mods = jnp.transpose(modulation[0], (1, 0, 2))
    head = jnp.transpose(w_head)
    scratch = [
        pltpu.VMEM((rows, prompts, model), bf16),
        pltpu.VMEM((txt, model), bf16),
        pltpu.VMEM(mods.shape, f32),
        pltpu.SMEM(text_lengths.shape, jnp.int32),
        pltpu.SMEM(timestep.shape, jnp.int32),
        pltpu.VMEM(latent.shape, f32),
        pltpu.VMEM(norm_gain.shape, f32),
        pltpu.VMEM(head.shape, bf16),
        pltpu.VMEM(w_qkv.shape, bf16), pltpu.VMEM(w_out.shape, bf16), pltpu.VMEM(w_out.shape, bf16),
        pltpu.VMEM(w_text_kv.shape, bf16),
        pltpu.VMEM(w_up.shape, bf16), pltpu.VMEM(w_down.shape, bf16),
        pltpu.VMEM((model // 128, own_rows, 128), f32),
        pltpu.VMEM((prompts, rows, model), bf16),
        pltpu.VMEM((2, prompts, rows, model), bf16),
        pltpu.VMEM((2, prompts, rows, model), bf16),
        pltpu.VMEM((txt_pad, model), f32),
        pltpu.VMEM((pairs, 2, own_rows, 128), bf16),
        pltpu.VMEM((pairs, 2, own_rows, 128), bf16),
        pltpu.VMEM((pairs, 2, own_rows, 128), bf16),
        pltpu.VMEM((pairs, txt_pad, 128), bf16),
        pltpu.VMEM((pairs, txt_pad, 128), bf16),
        pltpu.VMEM((2, pairs // 2, own_rows, 256), bf16),
        pltpu.VMEM((2, pairs // 2, own_rows, 256), bf16),
        pltpu.VMEM((pairs, 2, own_rows, 128), f32),
        pltpu.VMEM((prompts, rows, model), f32),
        pltpu.VMEM((prompts, rows, model), f32),
        pltpu.VMEM((prompts, rows, model), bf16),
        pltpu.VMEM((own_rows, units), bf16),
        pltpu.VMEM((2, prompts, rows, model), bf16),
        pltpu.VMEM((prompts, rows, model), bf16),
        pltpu.VMEM((2, rows, model), bf16),
        pltpu.VMEM((prompts, rows, 128), f32),
        pltpu.VMEM((prompts, rows, 128), f32),
        dma((8,)), dma((10,)), dma((prompts,)), dma((prompts,)), dma((prompts,)), dma((prompts,)),
        dma((20,)), dma((20,)), dma((pairs,)), dma((pairs,)), dma((prompts // 2,)), dma((prompts // 2,)),
        dma((prompts,)), dma((prompts,)), pltpu.SemaphoreType.REGULAR,
    ]
    stacked = pl.pallas_call(
        fused_kernel,
        out_shape=out,
        in_specs=[anym] * 13,
        out_specs=vmem,
        scratch_shapes=scratch,
        compiler_params=pltpu.CompilerParams(
            collective_id=0, has_side_effects=True, vmem_limit_bytes=60 << 20),
        name="fused_block",
    )(
        image_hidden[0], text_hidden[0], mods, text_lengths,
        timestep, latent, w_qkv, w_out, w_text_kv, norm_gain, w_up, w_down, head,
    )
    return stacked[0], stacked[1], stacked[2]


def solution(mesh):
    placed = (
        P("cfg", ("seq", "mlp"), None, None),
        P("cfg", "seq", None),
        P("cfg", None, None, None),
        P("cfg", None),
        P(),
        P(("seq", "mlp"), "cfg", None),
        P(None, None, "mlp"),
        P("mlp", None),
        P(None, None, "mlp"),
        P(),
        P(None, "mlp"),
        P("mlp", None),
        P(),
    )
    fits = mesh.shape["cfg"] == 2 and mesh.shape["seq"] == PROMPTS and mesh.shape["mlp"] == 2
    return jax.shard_map(
        fused_shards if fits else shards,
        mesh=mesh,
        in_specs=placed,
        out_specs=(
            P(("seq", "mlp"), "cfg", None),
            P(("seq", "mlp"), "cfg", None),
            P(("seq", "mlp"), "cfg", None),
        ),
        check_vma=False,
    )
```

```python
import math

import jax
import jax.numpy as jnp
from jax import lax
from jax.experimental import pallas as pl
from jax.experimental.pallas import tpu as pltpu
from jax.sharding import PartitionSpec as P

HEAD_DIM = 64
TXT = 154
STEPS = 28


EPS = 1e-06
GUIDE = 4.5
SHIFT = 3.0
PROMPTS = 8
PATCH = 64
MESH = pl.DeviceIdType.MESH


def partner_2(block, axis, stride):
    count = lax.axis_size(axis)
    route = []
    for low in range(count):
        high = low | 1 << stride
        if high != low and high < count:
            route += [(low, high), (high, low)]
    return lax.ppermute(block, axis, route)


def layer_norm(values):
    mean = jnp.mean(values, axis=-1, keepdims=True)
    centred = values - mean
    spread = jnp.mean(centred * centred, axis=-1, keepdims=True)
    return centred * lax.rsqrt(spread + EPS)


def modulate(values, shift, scale):
    return layer_norm(values) * (1.0 + scale) + shift


def head_norm(values, gain):
    shaped = values.reshape(values.shape[:-1] + (values.shape[-1] // HEAD_DIM, HEAD_DIM))
    square = jnp.mean(shaped * shaped, axis=-1, keepdims=True)
    return (shaped * lax.rsqrt(square + EPS) * gain).astype(jnp.bfloat16)


def sigma_of(index):
    level = 1.0 - index.astype(jnp.float32) / STEPS
    return SHIFT * level / (1.0 + (SHIFT - 1.0) * level)


def project_image(normed_rows, w_qkv, norm_gain):
    query = head_norm(
        jnp.einsum("tbd,de->tbe", normed_rows, w_qkv[0], preferred_element_type=jnp.float32),
        norm_gain[0],
    )
    keys = head_norm(
        jnp.einsum("tbd,de->tbe", normed_rows, w_qkv[1], preferred_element_type=jnp.float32),
        norm_gain[1],
    )
    values = jnp.einsum(
        "tbd,de->tbe", normed_rows, w_qkv[2], preferred_element_type=jnp.float32
    ).astype(jnp.bfloat16)
    flat_query = query.reshape(query.shape[:-2] + (-1,))
    flat_keys = keys.reshape(keys.shape[:-2] + (-1,))
    return jnp.concatenate([flat_query, flat_keys, values], axis=-1)


def key_terms(query, key_rows, value_rows, keep):
    factor = 1.0 / math.sqrt(HEAD_DIM)
    prompts = query.shape[1]
    if keep is None:
        keep = jnp.ones((prompts, key_rows.shape[0]), jnp.float32)

    def one_prompt(items):
        query_rows, keys_one, values_one, keep_one = items
        scores = (
            jnp.einsum("qhd,khd->hqk", query_rows, keys_one, preferred_element_type=jnp.float32)
            * factor
        )
        weights = jnp.exp(scores) * keep_one[None, None, :]
        numer = jnp.einsum(
            "hqk,khd->hqd",
            weights.astype(jnp.bfloat16),
            values_one,
            preferred_element_type=jnp.float32,
        )
        return (numer, jnp.sum(weights, axis=-1))

    return lax.map(
        one_prompt,
        (
            jnp.moveaxis(query, 1, 0),
            jnp.moveaxis(key_rows, 1, 0),
            jnp.moveaxis(value_rows, 1, 0),
            keep,
        ),
    )


def shards(
    image_hidden,
    text_hidden,
    modulation,
    text_lengths,
    timestep,
    latent,
    w_qkv,
    w_out,
    w_text_kv,
    norm_gain,
    w_up,
    w_down,
    w_head,
):
    mods = modulation[0]
    own_hidden = image_hidden[0]
    rows = own_hidden.shape[0]
    width = w_out.shape[0]
    heads = width // HEAD_DIM
    prompts = mods.shape[0]
    offset = lax.axis_index("mlp") * rows
    block_hidden = lax.all_gather(own_hidden, "mlp", axis=0, tiled=True).astype(jnp.float32)
    normed = modulate(block_hidden, mods[:, 0], mods[:, 1]).astype(jnp.bfloat16)
    projected = project_image(normed, w_qkv, norm_gain)
    block_rows = projected.shape[0]
    query = projected[..., :width].reshape(block_rows, prompts, heads, HEAD_DIM)
    own_pairs = projected[..., width:]
    text_rows = text_hidden.shape[1]
    position = lax.axis_index("seq") * text_rows + lax.iota(jnp.int32, text_rows)
    owner = position // TXT
    pick = (owner[:, None] == lax.iota(jnp.int32, prompts)[None, :]).astype(jnp.float32)
    text_shift = jnp.dot(pick, mods[:, 6], precision=lax.Precision.HIGHEST)
    text_scale = jnp.dot(pick, mods[:, 7], precision=lax.Precision.HIGHEST)
    text_normed = modulate(text_hidden[0].astype(jnp.float32), text_shift, text_scale).astype(
        jnp.bfloat16
    )
    text_keys = head_norm(
        jnp.dot(text_normed, w_text_kv[0], preferred_element_type=jnp.float32), norm_gain[2]
    )
    text_keys = text_keys.reshape(text_rows, width)
    text_values = jnp.dot(text_normed, w_text_kv[1], preferred_element_type=jnp.float32).astype(
        jnp.bfloat16
    )
    text_pairs = jnp.concatenate([text_keys, text_values], axis=-1)
    keep = (lax.iota(jnp.int32, TXT)[None, :] < text_lengths[0][:, None]).astype(jnp.float32)

    def split_pairs(pairs):
        shape = pairs.shape[:2] + (heads, HEAD_DIM)
        return (pairs[..., :width].reshape(shape), pairs[..., width:].reshape(shape))

    all_image, all_text = (
        lax.all_gather(own_pairs, "seq", axis=0, tiled=True),
        lax.all_gather(text_pairs, "seq", axis=0, tiled=True),
    )
    shaped = jnp.transpose(all_text.reshape(prompts, TXT, 2 * width), (1, 0, 2))
    key_rows, value_rows = split_pairs(shaped)
    text_numer, text_denom = key_terms(query, key_rows, value_rows, keep)
    key_rows, value_rows = split_pairs(all_image)
    image_numer, image_denom = key_terms(query, key_rows, value_rows, None)
    numer = text_numer + image_numer
    denom = text_denom + image_denom
    attended = (numer / denom[..., None]).astype(jnp.bfloat16)
    attended = jnp.transpose(attended, (2, 0, 1, 3)).reshape(block_rows, prompts, width)
    part = attended
    attention_out = lax.psum(
        jnp.einsum("tbe,ed->tbd", part, w_out, preferred_element_type=jnp.float32).astype(
            jnp.bfloat16
        ),
        "mlp",
    ).astype(jnp.float32)
    first = block_hidden + mods[:, 2] * attention_out
    mlp_in = modulate(first, mods[:, 3], mods[:, 4]).astype(jnp.bfloat16)
    raised = jnp.einsum("tbd,du->tbu", mlp_in, w_up, preferred_element_type=jnp.float32)
    activated = jax.nn.gelu(raised, approximate=True).astype(jnp.bfloat16)
    own_first = lax.dynamic_slice_in_dim(first, offset, rows, 0)
    part = activated
    mlp_out = lax.psum_scatter(
        jnp.einsum("tbu,ud->tbd", part, w_down, preferred_element_type=jnp.float32).astype(
            jnp.bfloat16
        ),
        "mlp",
        scatter_dimension=0,
        tiled=True,
    ).astype(jnp.float32)
    second = own_first + mods[:, 5] * mlp_out
    final = modulate(second, mods[:, 8], mods[:, 9]).astype(jnp.bfloat16)
    own_velocity = jnp.einsum("tbd,dp->tbp", final, w_head, preferred_element_type=jnp.float32)
    half_count = prompts // 2
    branch = lax.axis_index("cfg")
    outgoing = lax.dynamic_slice_in_dim(own_velocity, (1 - branch) * half_count, half_count, 1)
    kept = lax.dynamic_slice_in_dim(own_velocity, branch * half_count, half_count, 1)
    partner = partner_2(outgoing, "cfg", 0)
    is_conditional = branch == 0
    conditional = jnp.where(is_conditional, kept, partner)
    unconditional = jnp.where(is_conditional, partner, kept)
    velocity = unconditional + GUIDE * (conditional - unconditional)
    sigma_now = sigma_of(timestep[0])
    sigma_after = sigma_of(timestep[0] + 1)
    next_latent = latent + (sigma_after - sigma_now) * velocity
    denoised = latent - sigma_now * velocity
    return (velocity, next_latent, denoised)

def fused_kernel(
    hid_hbm, text_hbm, mod_hbm, len_hbm, step_hbm, latent_hbm, wqkv_hbm, wout_hbm, wtext_hbm,
    gain_hbm, wup_hbm, wdown_hbm, whead_hbm,
    out_ref,
    hid_ref, text_ref, mod_ref, len_ref, step_ref, latent_ref, gain_ref, whead_ref,
    wqkv, wout, wout_far, wtext, wup, wdown,
    wide, ready, gathered, normed, text_norm, q6, k6, v6, kt6, vt6, attended, att_in,
    early, proj, first_buf, mlp_in, act, down, down_in, final, half_out, half_in,
    isem, wsem, a2a_send, a2a_recv, fwd_send, fwd_recv, far_send, far_recv, at_send, at_recv,
    dn_send, dn_recv, out_send, out_recv, go_sem,
):
    c = lax.axis_index("cfg")
    s = lax.axis_index("seq")
    m = lax.axis_index("mlp")
    other = 1 - m
    ring = PROMPTS
    rows = hid_ref.shape[0]
    own_rows = rows * ring
    width = wout.shape[0]
    model = wout.shape[1]
    units = wup.shape[1]
    pairs = width // 128
    txt_pad = text_norm.shape[0]
    txt = text_ref.shape[0]
    f32, bf16 = jnp.float32, jnp.bfloat16
    partner = (c, s, other)
    sibling = (1 - c, s, m)

    bits = (lax.rem(s, 2), lax.rem(s // 2, 2), s // 4)

    def peer(k):
        return sum(((1 - bits[i]) if (k >> i) & 1 else bits[i]) * (1 << i) for i in range(3))

    inputs = []
    for i, (src, dst) in enumerate((
        (hid_hbm, hid_ref), (text_hbm, text_ref), (mod_hbm, mod_ref), (gain_hbm, gain_ref),
        (len_hbm, len_ref), (step_hbm, step_ref), (latent_hbm, latent_ref), (whead_hbm, whead_ref),
    )):
        inputs.append(pltpu.make_async_copy(src, dst, isem.at[i]))
    inputs[0].start()

    barrier = pltpu.get_barrier_semaphore()
    lead = c == 0
    tail_core = c == 1
    pl.semaphore_signal(barrier, inc=1, device_id=partner, device_id_type=MESH)

    @pl.when(lead)
    def _():
        pl.semaphore_signal(barrier, inc=1, device_id=sibling, device_id_type=MESH)

    for k in range(1, ring):
        pl.semaphore_signal(barrier, inc=1, device_id=(1, peer(k), m), device_id_type=MESH)

    for cp in inputs[1:]:
        cp.start()
    loads = []
    jobs = [(wtext_hbm.at[i], wtext.at[i]) for i in range(2)]
    jobs += [(wqkv_hbm.at[i], wqkv.at[i]) for i in range(3)]
    jobs += [(wout_hbm, wout)]
    jobs += [(wup_hbm.at[pl.ds(i * model // 2, model // 2)], wup.at[pl.ds(i * model // 2, model // 2)]) for i in range(2)]
    jobs += [(wdown_hbm.at[pl.ds(i * units // 2, units // 2)], wdown.at[pl.ds(i * units // 2, units // 2)]) for i in range(2)]
    for i, (src, dst) in enumerate(jobs):
        loads.append(pltpu.make_async_copy(src, dst, wsem.at[i]))
    for cp in loads[:2]:
        cp.start()

    inputs[0].wait()
    lanes = model // 128
    for j in range(lanes):
        tile = hid_ref[:, :, j * 128 : (j + 1) * 128]
        wide[j] = tile.astype(f32).reshape(own_rows, 128)
    for p in range(ring):
        for j in range(lanes):
            ready[p, :, j * 128 : (j + 1) * 128] = wide[j, pl.ds(p, rows, stride=ring), :].astype(bf16)
    sends = []

    def remote(src, dst, ssem, rsem, dev):
        return pltpu.make_async_remote_copy(
            src_ref=src, dst_ref=dst, send_sem=ssem, recv_sem=rsem,
            device_id=dev, device_id_type=MESH)

    def send(src, dst, ssem, rsem, dev):
        sends.append(remote(src, dst, ssem, rsem, dev))
        sends[-1].start()

    def arrive(dst, ssem, rsem, dev):
        pltpu.make_async_remote_copy(
            src_ref=dst, dst_ref=dst, send_sem=ssem, recv_sem=rsem,
            device_id=dev, device_id_type=MESH).wait_recv()

    lead_sends, tail_sends = [], []
    quarter = 4
    piece = width // (4 * quarter)

    def far_rows(core, j, i):
        q0 = (1 - bits[0]) if j & 1 else bits[0]
        q1 = (1 - bits[1]) if j & 2 else bits[1]
        start = (((q0 + 2 * q1) * 2 + core) * 2 + i) * piece
        return pl.ds(pl.multiple_of(start, 16), piece)

    near_y = (c, peer(1), m)
    near_z = (c, peer(2), m)

    def far_copy(at, i, n, dev, src=None):
        src = wout_far if src is None else src
        return remote(src.at[at], wout_far.at[at], far_send.at[i], far_recv.at[n], dev)

    def far_send_to(at, i, dev):
        sends.append(far_copy(at, i, i, dev))
        sends[-1].start()

    def far_arrive(at, i, dev):
        far_copy(at, i, i, dev).wait_recv()

    def far_cross():
        crossing = [
            far_copy(far_rows(core, 0, i), 16 * core + i, 16 * core + i, partner, wout_hbm)
            for i in range(2) for core in range(2)]
        lead_sends.extend(crossing)

        @pl.when(lead)
        def _():
            pl.semaphore_wait(barrier, 1)
            for cp in crossing:
                cp.start()

    def far_own_lead(i):
        own, near = far_rows(0, 0, i), far_rows(1, 0, i)
        first = [
            far_copy(own, 4 + i, 4 + i, near_z), far_copy(own, 2 + i, 2 + i, near_y),
            far_copy(own, 8 + i, 8 + i, sibling)]
        second = far_copy(near, 18 + i, i, sibling)
        lead_sends.extend(first + [second])

        @pl.when(lead)
        def _():
            far_arrive(own, i, partner)
            for cp in first:
                cp.start()
            far_arrive(near, 16 + i, partner)
            second.start()

    def far_own_tail(i):
        own = far_rows(1, 0, i)
        copies = [far_copy(own, 4 + i, 4 + i, near_z), far_copy(own, 2 + i, 2 + i, near_y)]
        tail_sends.extend(copies)

        @pl.when(tail_core)
        def _():
            far_arrive(own, i, sibling)
            for cp in copies:
                cp.start()

    def far_from_y(i):
        at = far_rows(c, 1, i)
        far_arrive(at, 2 + i, near_y)
        if i == 0:
            far_send_to(at, 6, near_z)
        far_send_to(at, 10 + i, sibling)

    def far_from_z(i):
        at = far_rows(c, 2, i)
        far_arrive(at, 4 + i, near_z)
        if i == 1:
            far_send_to(at, 7, near_y)
        far_send_to(at, 12 + i, sibling)

    def far_corner(i):
        at = far_rows(c, 3, i)
        far_arrive(at, 6 + i, near_z if i == 0 else near_y)
        far_send_to(at, 14 + i, sibling)

    def far_done():
        @pl.when(tail_core)
        def _():
            for i in range(2):
                far_arrive(far_rows(0, 0, i), 8 + i, sibling)

        for t in range(2, 8):
            far_arrive(far_rows(1 - c, t // 2, t % 2), 8 + t, sibling)

    gathered[m, s] = ready[s]
    far_cross()
    for cp in inputs[1:]:
        cp.wait()
    for cp in loads[2:5]:
        cp.start()

    def mod_row(k):
        return mod_ref[k, pl.ds(s, 1), :]

    def norm_rows(values, k):
        mean = jnp.mean(values, axis=-1, keepdims=True)
        centred = values - mean
        spread = jnp.mean(centred * centred, axis=-1, keepdims=True)
        return centred * lax.rsqrt(spread + EPS) * (1.0 + mod_row(k + 1)) + mod_row(k)

    whole_blocks = txt // 16

    def text_block(i, carry):
        at = pl.ds(pl.multiple_of(i * 16, 16), 16)
        text_norm[at, :] = norm_rows(text_ref[at, :].astype(f32), 6)
        return carry

    lax.fori_loop(0, whole_blocks, text_block, 0, unroll=3 if whole_blocks % 3 == 0 else 1)
    tail = txt - whole_blocks * 16
    if tail:
        text_norm[whole_blocks * 16 : txt, :] = norm_rows(
            text_ref[whole_blocks * 16 : txt, :].astype(f32), 6)
    if txt_pad > txt:
        text_norm[txt:txt_pad, :] = jnp.zeros((txt_pad - txt, model), f32)

    row_id = lax.broadcasted_iota(jnp.int32, (256, 256), 0)
    col_id = lax.broadcasted_iota(jnp.int32, (256, 256), 1)
    same_head = ((row_id // HEAD_DIM) == (col_id // HEAD_DIM)).astype(f32).astype(bf16)

    def square_sums(u):
        return jnp.dot((u * u).astype(bf16), same_head, preferred_element_type=f32)

    def gain_of(i):
        one = gain_ref[i : i + 1, :]
        return jnp.concatenate([one] * 4, axis=1)

    keep = (lax.broadcasted_iota(jnp.int32, (txt_pad, 128), 0) < len_ref[0, s]).astype(f32).astype(bf16)
    lane = lax.broadcasted_iota(jnp.int32, (1, 128), 1)
    low_lane = (lane < HEAD_DIM).astype(f32).astype(bf16)
    high_lane = (lane >= HEAD_DIM).astype(f32).astype(bf16)

    def project(lhs, weight, gain, mask, store):
        blocks = [
            jnp.dot(lhs, weight[:, j * 256 : (j + 1) * 256], preferred_element_type=f32)
            for j in range(width // 256)]
        if gain is not None:
            totals = [square_sums(u) for u in blocks]
            blocks = [
                u * lax.rsqrt(total * (1.0 / HEAD_DIM) + EPS) * gain
                for u, total in zip(blocks, totals)]
        for j, u in enumerate(blocks):
            for t in range(2):
                res = u[:, t * 128 : (t + 1) * 128].astype(bf16)
                store(2 * j + t, res if mask is None else res * mask)

    def to_text(buf):
        def store(i, value):
            buf[i] = value

        return store

    def to_half(buf, half):
        def store(i, value):
            buf[i, half] = value

        return store

    text_lhs = text_norm[...].astype(bf16)

    @pl.when(tail_core)
    def _():
        pl.semaphore_wait(barrier, 2 * ring)
        pl.semaphore_signal(go_sem, inc=1, device_id=sibling, device_id_type=MESH)

    @pl.when(lead)
    def _():
        pl.semaphore_wait(go_sem, 1)


    for k in (4, 5, 6, 7, 2, 3, 1):
        send(ready.at[peer(k)], gathered.at[m, s], a2a_send.at[k], a2a_recv.at[k], (c, peer(k), m))

    loads[0].wait()
    project(text_lhs, wtext.at[0], gain_of(2), None, to_text(kt6))
    loads[1].wait()
    project(text_lhs, wtext.at[1], None, keep, to_text(vt6))

    def forward(k):
        src = peer(k)
        if k:
            arrive(gathered.at[m, src], a2a_send.at[k], a2a_recv.at[k], (c, src, m))
        send(gathered.at[m, src], gathered.at[m, src], fwd_send.at[k], fwd_recv.at[k], partner)

    forward(0)
    for cp in loads[5:]:
        cp.start()

    def dot_t(a, b):
        return lax.dot_general(a, b, (((1,), (1,)), ((), ())), preferred_element_type=f32)

    sides = ((low_lane, high_lane), (high_lane, low_lane))

    def image_part(qh, p, half, mine, rest):
        w_img = jnp.exp(dot_t(qh, k6[p, half])).astype(bf16)
        return jnp.dot(w_img, v6[p, half] * mine + rest, preferred_element_type=f32)

    def text_part(qh, p, mine, rest):
        w_txt = jnp.exp(dot_t(qh, kt6[p])).astype(bf16)
        return jnp.dot(w_txt, vt6[p] * mine + keep * rest, preferred_element_type=f32)

    def attend_early():
        for p in range(pairs):
            q = q6[p, m]
            for n, (mine, rest) in enumerate(sides):
                qh = q * mine
                early[p, n] = image_part(qh, p, m, mine, rest) + text_part(qh, p, mine, rest)

    def attend_pair(half, p, begun):
        q = q6[p, half]
        outs = []
        for n, (mine, rest) in enumerate(sides):
            qh = q * mine
            if begun:
                outs.append(early[p, n] + image_part(qh, p, other, mine, rest))
                continue
            k = k6[p].reshape(2 * own_rows, 128)
            v = v6[p].reshape(2 * own_rows, 128)
            w_img = jnp.exp(dot_t(qh, k)).astype(bf16)
            outs.append(
                jnp.dot(w_img, v * mine + rest, preferred_element_type=f32)
                + text_part(qh, p, mine, rest))
        numer = jnp.where(lane < HEAD_DIM, outs[0], outs[1])
        denom = pltpu.roll(jnp.where(lane < HEAD_DIM, outs[1], outs[0]), HEAD_DIM, 1)
        attended[half, p // 2, :, (p % 2) * 128 : (p % 2 + 1) * 128] = (numer / denom).astype(bf16)

    def norm_blocks(half, first_at, count):
        def block(i, carry):
            normed[half, first_at + i] = norm_rows(gathered[half, first_at + i].astype(f32), 0).astype(bf16)
            return carry

        lax.fori_loop(0, count, block, 0, unroll=count)

    q_gain = gain_of(0) * (1.0 / math.sqrt(HEAD_DIM))
    k_gain = gain_of(1)

    def project_rows(half, which):
        lhs = normed[half].reshape(own_rows, model)
        buf, gain = ((q6, q_gain), (k6, k_gain), (v6, None))[which]
        project(lhs, wqkv.at[which], gain, None, to_half(buf, half))

    forward(1)
    far_own_lead(0)
    far_own_lead(1)
    forward(2)
    far_own_tail(0)
    forward(3)
    forward(4)
    far_own_tail(1)
    forward(5)
    forward(6)
    forward(7)
    norm_blocks(m, 0, ring)
    for i in (2, 3, 4):
        loads[i].wait()
    project_rows(m, 1)
    project_rows(m, 2)
    project_rows(m, 0)
    attend_early()
    far_from_y(0)
    far_from_z(0)

    for k in range(ring):
        src = peer(k)
        arrive(gathered.at[other, src], fwd_send.at[k], fwd_recv.at[k], partner)
    norm_blocks(other, 0, ring)
    project_rows(other, 1)
    project_rows(other, 2)
    far_from_y(1)
    far_from_z(1)

    def attend(half, base):
        for g in range(pairs // 2):
            for p in (2 * g, 2 * g + 1):
                attend_pair(half, p, base == 0)
            send(attended.at[half, g], att_in.at[half, g],
                 at_send.at[base + g], at_recv.at[base + g], partner)

    def att_arrive(half, base):
        for g in range(pairs // 2):
            arrive(att_in.at[half, g], at_send.at[base + g], at_recv.at[base + g], partner)

    attend(m, 0)
    far_corner(0)
    project_rows(other, 0)
    far_corner(1)
    attend(other, pairs // 2)
    loads[5].wait()

    def out_rows(half):
        mine = jnp.concatenate([attended[half, g] for g in range(pairs // 2)], axis=1)
        far = jnp.concatenate([att_in[half, g] for g in range(pairs // 2)], axis=1)
        for j in range(model // 512):
            cols = slice(j * 512, (j + 1) * 512)
            res = jnp.dot(mine, wout[:, cols], preferred_element_type=f32)
            res = res + jnp.dot(far, wout_far[:, cols], preferred_element_type=f32)
            proj[:, :, cols] = res.reshape(ring, rows, 512)

    def first_rows(half, hold):
        def block(i, carry):
            first = gathered[half, i].astype(f32) + mod_row(2) * proj[i]
            if hold:
                first_buf[i] = first
            mlp_in[i] = norm_rows(first, 3).astype(bf16)
            return carry

        lax.fori_loop(0, ring, block, 0, unroll=ring)

    def up():
        lhs = mlp_in[...].reshape(own_rows, model)
        for j in range(units // 512):
            cols = slice(j * 512, (j + 1) * 512)
            r = jnp.dot(lhs, wup[:, cols], preferred_element_type=f32)
            inner = math.sqrt(2.0 / math.pi) * (r + 0.044715 * (r * r * r))
            act[:, cols] = (0.5 * r * (1.0 + jnp.tanh(inner))).astype(bf16)

    def down_rows(half):
        lhs = act[...]
        for j in range(model // 512):
            cols = slice(j * 512, (j + 1) * 512)
            res = jnp.dot(lhs, wdown[:, cols], preferred_element_type=f32).astype(bf16)
            down[half, :, :, cols] = res.reshape(ring, rows, 512)

    couples = ring // 2

    def couple_at(t):
        b1 = (1 - bits[1]) if t & 1 else bits[1]
        b2 = (1 - bits[2]) if t & 2 else bits[2]
        return 2 * b1 + 4 * b2

    order = tuple(range(couples - 1, -1, -1))

    att_arrive(other, 0)
    far_done()
    out_rows(other)
    first_rows(other, False)
    for i in (6, 7):
        loads[i].wait()
    up()
    for i in (8, 9):
        loads[i].wait()
    down_rows(other)
    for t in order:
        at = pl.ds(couple_at(t), 2)
        send(down.at[other, at], down_in.at[at], dn_send.at[t], dn_recv.at[t], partner)
    att_arrive(m, pairs // 2)
    out_rows(m)
    first_rows(m, True)
    up()
    down_rows(m)

    head = whead_ref[...]
    heads2 = jnp.concatenate([head, head], axis=0)
    home = s // (ring // 2)
    slot = c * (ring // 2) + lax.rem(s, ring // 2)
    at_home = c == home
    outs = []
    for t in order:
        start = couple_at(t)
        at = pl.ds(start, 2)
        arrive(down_in.at[at], dn_send.at[t], dn_recv.at[t], partner)
        for e in range(2):
            i = start + e
            total = down[m, i].astype(f32) + down_in[i].astype(f32)
            second = first_buf[i] + mod_row(5) * total
            final[e] = norm_rows(second, 8).astype(bf16)
        hv = dot_t(final[...].reshape(2 * rows, model), heads2)
        for e in range(2):
            dest = start + e
            half_out[dest] = hv[e * rows : (e + 1) * rows]
            cp = pltpu.make_async_remote_copy(
                src_ref=half_out.at[dest], dst_ref=half_in.at[slot],
                send_sem=out_send.at[2 * t + e], recv_sem=out_recv.at[slot],
                device_id=(home, dest, m), device_id_type=MESH)
            if t:
                cp.start()
                sends.append(cp)
                continue
            stays = jnp.logical_and(at_home, s == dest)
            outs.append((cp, stays))

            @pl.when(jnp.logical_not(stays))
            def _(cp=cp):
                cp.start()

            @pl.when(stays)
            def _(dest=dest):
                half_in[slot] = half_out[dest]

    for q in range(ring):
        branch, local = q // (ring // 2), q % (ring // 2)
        prompt = c * (ring // 2) + local
        is_self = jnp.logical_and(c == branch, s == prompt)

        @pl.when(jnp.logical_not(is_self))
        def _():
            pltpu.make_async_remote_copy(
                src_ref=half_out.at[0], dst_ref=half_in.at[q],
                send_sem=out_send.at[0], recv_sem=out_recv.at[q],
                device_id=(branch, prompt, m), device_id_type=MESH).wait_recv()

    t = jnp.full((1, PATCH), step_ref[0], jnp.int32)

    def sigma(index):
        level = 1.0 - index.astype(f32) / STEPS
        return SHIFT * level / (1.0 + (SHIFT - 1.0) * level)

    now, after = sigma(t), sigma(t + 1)
    for p in range(ring // 2):
        cond = half_in[p][:, :PATCH]
        uncond = half_in[ring // 2 + p][:, :PATCH]
        velocity = uncond + GUIDE * (cond - uncond)
        base = latent_ref[:, p, :]
        out_ref[0, :, p, :] = velocity
        out_ref[1, :, p, :] = base + (after - now) * velocity
        out_ref[2, :, p, :] = base - now * velocity

    for cp in sends:
        cp.wait_send()

    @pl.when(lead)
    def _():
        for cp in lead_sends:
            cp.wait_send()

    @pl.when(tail_core)
    def _():
        for cp in tail_sends:
            cp.wait_send()

    for cp, stays in outs:
        @pl.when(jnp.logical_not(stays))
        def _(cp=cp):
            cp.wait_send()


def fused_shards(
    image_hidden, text_hidden, modulation, text_lengths, timestep, latent,
    w_qkv, w_out, w_text_kv, norm_gain, w_up, w_down, w_head,
):
    f32, bf16 = jnp.float32, jnp.bfloat16
    rows, prompts, model = image_hidden.shape[1:]
    txt = text_hidden.shape[1]
    txt_pad = -(-txt // 16) * 16
    width = w_out.shape[0]
    units = w_up.shape[1]
    own_rows = rows * prompts
    pairs = width // 128
    vmem = pl.BlockSpec(memory_space=pltpu.VMEM)
    anym = pl.BlockSpec(memory_space=pl.ANY)
    dma = pltpu.SemaphoreType.DMA
    out = jax.ShapeDtypeStruct((3,) + latent.shape, f32)
    mods = jnp.transpose(modulation[0], (1, 0, 2))
    head = jnp.transpose(w_head)
    scratch = [
        pltpu.VMEM((rows, prompts, model), bf16),
        pltpu.VMEM((txt, model), bf16),
        pltpu.VMEM(mods.shape, f32),
        pltpu.SMEM(text_lengths.shape, jnp.int32),
        pltpu.SMEM(timestep.shape, jnp.int32),
        pltpu.VMEM(latent.shape, f32),
        pltpu.VMEM(norm_gain.shape, f32),
        pltpu.VMEM(head.shape, bf16),
        pltpu.VMEM(w_qkv.shape, bf16), pltpu.VMEM(w_out.shape, bf16), pltpu.VMEM(w_out.shape, bf16),
        pltpu.VMEM(w_text_kv.shape, bf16),
        pltpu.VMEM(w_up.shape, bf16), pltpu.VMEM(w_down.shape, bf16),
        pltpu.VMEM((model // 128, own_rows, 128), f32),
        pltpu.VMEM((prompts, rows, model), bf16),
        pltpu.VMEM((2, prompts, rows, model), bf16),
        pltpu.VMEM((2, prompts, rows, model), bf16),
        pltpu.VMEM((txt_pad, model), f32),
        pltpu.VMEM((pairs, 2, own_rows, 128), bf16),
        pltpu.VMEM((pairs, 2, own_rows, 128), bf16),
        pltpu.VMEM((pairs, 2, own_rows, 128), bf16),
        pltpu.VMEM((pairs, txt_pad, 128), bf16),
        pltpu.VMEM((pairs, txt_pad, 128), bf16),
        pltpu.VMEM((2, pairs // 2, own_rows, 256), bf16),
        pltpu.VMEM((2, pairs // 2, own_rows, 256), bf16),
        pltpu.VMEM((pairs, 2, own_rows, 128), f32),
        pltpu.VMEM((prompts, rows, model), f32),
        pltpu.VMEM((prompts, rows, model), f32),
        pltpu.VMEM((prompts, rows, model), bf16),
        pltpu.VMEM((own_rows, units), bf16),
        pltpu.VMEM((2, prompts, rows, model), bf16),
        pltpu.VMEM((prompts, rows, model), bf16),
        pltpu.VMEM((2, rows, model), bf16),
        pltpu.VMEM((prompts, rows, 128), f32),
        pltpu.VMEM((prompts, rows, 128), f32),
        dma((8,)), dma((10,)), dma((prompts,)), dma((prompts,)), dma((prompts,)), dma((prompts,)),
        dma((20,)), dma((20,)), dma((pairs,)), dma((pairs,)), dma((prompts // 2,)), dma((prompts // 2,)),
        dma((prompts,)), dma((prompts,)), pltpu.SemaphoreType.REGULAR,
    ]
    stacked = pl.pallas_call(
        fused_kernel,
        out_shape=out,
        in_specs=[anym] * 13,
        out_specs=vmem,
        scratch_shapes=scratch,
        compiler_params=pltpu.CompilerParams(
            collective_id=0, has_side_effects=True, vmem_limit_bytes=60 << 20),
        name="fused_block",
    )(
        image_hidden[0], text_hidden[0], mods, text_lengths,
        timestep, latent, w_qkv, w_out, w_text_kv, norm_gain, w_up, w_down, head,
    )
    return stacked[0], stacked[1], stacked[2]


def solution(mesh):
    placed = (
        P("cfg", ("seq", "mlp"), None, None),
        P("cfg", "seq", None),
        P("cfg", None, None, None),
        P("cfg", None),
        P(),
        P(("seq", "mlp"), "cfg", None),
        P(None, None, "mlp"),
        P("mlp", None),
        P(None, None, "mlp"),
        P(),
        P(None, "mlp"),
        P("mlp", None),
        P(),
    )
    fits = mesh.shape["cfg"] == 2 and mesh.shape["seq"] == PROMPTS and mesh.shape["mlp"] == 2
    return jax.shard_map(
        fused_shards if fits else shards,
        mesh=mesh,
        in_specs=placed,
        out_specs=(
            P(("seq", "mlp"), "cfg", None),
            P(("seq", "mlp"), "cfg", None),
            P(("seq", "mlp"), "cfg", None),
        ),
        check_vma=False,
    )
```
